32 devices in a mesh: gx: 8 (over z, x), gy: 4 (over y, core).
Axes of the slice: x: 2, y: 2, z: 4, core: 2. Of those that a mesh axis runs over, the one named last changes fastest.
Arguments:
- activations: bfloat16 [64, 65536], P('gx', 'gy'), may hold values from -6 to 6
- live_blocks: int32 [4, 8, 512], P(None, 'gx', 'gy'), may hold values 0 or 1
- tile_index: int32 [4, 512, 8], replicated, may hold values from 0 to 511, as said below
- tile_count: int32 [4, 4, 128], P(None, 'gy', 'gx'), may hold values from 1 to 8, as said below
- weight_tiles: bfloat16 [4, 4, 128, 8, 128, 128], P(None, 'gy', 'gx'), may hold values from -0.375 to 0.375
- bias_terms: float32 [4, 4, 128, 128], P(None, 'gy', 'gx'), may hold values from -2 to 2
Outputs:
- final_layer: bfloat16 [64, 65536], P('gx', 'gy')
The draws below stay inside these ranges and needn't reach their ends.
Inputs may be any that keep to these rules, and one draw needn't show every extreme that they name: The input block of slot t lies in group t mod 4: tile_index[l, j, t] divided by 128, rounded down, equals t mod 4. Of the 16 blocks g * 128 + r * 16 + k (k < 16) held by the device with index r of gx and g of gy, at most one has tile_count above 4 in each layer; in every layer some device has such a block with exactly 8 used slots.
All inputs are finite; a program needn't handle non-finite values. No bound on the sum of `live_blocks` on one device may be relied on, other than what follows from the above.
Results may differ from the reference program's by a relative error of at most 0.0057.
Values may be sent and summed in bfloat16 or wider, within the bound.
No kernel may reach another device: no remote copies, remote signals or barrier semaphores. Data moves between devices by JAX's collectives and lax.ppermute only.
A program may use at most 64 MiB of HBM per device.

```python
import jax
import jax.numpy as jnp
from jax import lax

NEUR = 65536
BLK = 128
TILES = 8
LAYERS = 4
ROWS_DEV = 8
GROUPS = 4
RGROUPS = 8
NBLK = 512
GBLK = 128
OWN = 16
ROWS = 64


def draw_tile_index(key, part):
    tile_pos = jnp.arange(TILES, dtype=jnp.int32)
    base = tile_pos % GROUPS * GBLK
    offsets = jax.random.randint(key, (LAYERS, NBLK, TILES), 0, GBLK, dtype=jnp.int32)
    return (base[None, None, :] + offsets).astype(jnp.int32)


def draw_tile_count(key, part):
    key_hot = jax.random.fold_in(key, 11)
    key_light = jax.random.fold_in(key, 12)
    key_heavy = jax.random.fold_in(key, 13)
    key_place = jax.random.fold_in(key, 14)
    hot = jax.random.randint(key_hot, (LAYERS, GROUPS, RGROUPS, 1), 0, 4, dtype=jnp.int32) == 0
    first = (jnp.arange(GROUPS)[:, None, None] == 0) & (jnp.arange(RGROUPS)[None, :, None] == 0)
    hot = hot | first[None]
    light = jax.random.randint(key_light, (LAYERS, GROUPS, RGROUPS, OWN), 1, GROUPS + 1, dtype=jnp.int32)
    heavy = jax.random.randint(key_heavy, (LAYERS, GROUPS, RGROUPS, 1), GROUPS + 1, TILES + 1, dtype=jnp.int32)
    heavy = jnp.where(first[None], TILES, heavy)
    place = jax.random.randint(key_place, (LAYERS, GROUPS, RGROUPS, 1), 0, OWN, dtype=jnp.int32)
    chosen = hot & (jnp.arange(OWN, dtype=jnp.int32)[None, None, None, :] == place)
    counts = jnp.where(chosen, heavy, light)
    return counts.reshape(LAYERS, GROUPS, GBLK).astype(jnp.int32)


def with_ends(result, rng, smallest, largest):
    longest = result.shape.index(max(result.shape))
    spots = []
    for shift in (0, 1):
        where = [jax.random.randint(jax.random.fold_in(rng, axis), (), 0, length) for axis, length in enumerate(result.shape)]
        where[longest] = (where[longest] + shift) % result.shape[longest]
        spots.append(tuple(where))
    return result.at[spots[0]].set(smallest).at[spots[1]].set(largest)


def shard_levels(own_key, extent, split, low, high):
    gain = 1.0
    for dim, shards_of in split:
        heights = jax.random.uniform(jax.random.fold_in(jax.random.fold_in(own_key, 6), dim), (shards_of,), jnp.float32, low / len(split), high / len(split))
        gain = gain * jnp.repeat(jnp.exp(heights), extent[dim] // shards_of).reshape((-1,) + (1,) * (len(extent) - 1 - dim))
    return gain


def noise(own_key, dims, deviation, reach, split=(), kind=jnp.bfloat16):
    level = shard_levels(own_key, dims, split, -0.22, 0.18) if split else 1.0
    drawn = jax.random.normal(own_key, dims, jnp.float32) * deviation * level
    return jnp.minimum(jnp.maximum(drawn, -reach), reach).astype(kind)


def setup_inputs(seed: int = 0) -> dict:
    streams_of = jax.random.split(jax.random.key(seed), 7)
    activations = noise(streams_of[0], (ROWS, NEUR), 1.0, 6.0, ((0, 8), (1, 4)))
    live_blocks = with_ends((jax.random.randint(streams_of[1], (LAYERS, RGROUPS, NBLK), 0, 4) < 3).astype(jnp.int32), jax.random.fold_in(streams_of[1], 1), 0, 1)
    tile_index = draw_tile_index(jax.random.fold_in(streams_of[6], 71), 0)
    tile_count = draw_tile_count(jax.random.fold_in(streams_of[6], 71), 0)
    weight_tiles = noise(streams_of[4], (LAYERS, GROUPS, GBLK, TILES, BLK, BLK), (2 * BLK) ** -0.5, 0.375, ((1, 4), (2, 8)))
    bias_terms = noise(streams_of[5], (LAYERS, GROUPS, GBLK, BLK), 0.3, 2.0, ((1, 4), (2, 8)), jnp.float32)
    return {"activations": activations, "live_blocks": live_blocks, "tile_index": tile_index, "tile_count": tile_count, "weight_tiles": weight_tiles, "bias_terms": bias_terms}


batch_blocks = 16


def reference(activations, live_blocks, tile_index, tile_count, weight_tiles, bias_terms):
    current = activations
    total_rows = activations.shape[0]
    batches = NBLK // batch_blocks
    for layer_index in range(LAYERS):
        kept_mask = jnp.repeat(live_blocks[layer_index].astype(jnp.bfloat16), ROWS_DEV, axis=0)
        blocks = current.reshape(total_rows, NBLK, BLK) * kept_mask[:, :, None]
        usable = (jnp.arange(TILES, dtype=jnp.int32)[None, :] < tile_count[layer_index].reshape(NBLK)[:, None]).astype(jnp.float32)
        tile_ids = tile_index[layer_index].reshape(batches, batch_blocks * TILES).astype(jnp.int32)
        weights = weight_tiles[layer_index].reshape(batches, batch_blocks, TILES, BLK, BLK)
        usable = usable.reshape(batches, batch_blocks, TILES)
        offsets = bias_terms[layer_index].reshape(batches, batch_blocks, BLK)

        def one_batch(pieces):
            picked_ids, weight_part, usable_part, offset_part = pieces
            gathered = jnp.take(blocks, picked_ids, axis=1).reshape(total_rows, batch_blocks, TILES, BLK).astype(jnp.float32)
            masked = weight_part.astype(jnp.float32) * usable_part[:, :, None, None]
            summed = jnp.einsum("rkti,ktij->rkj", gathered, masked, precision=lax.Precision.HIGHEST)
            return jax.nn.relu(summed + offset_part[None]).astype(jnp.bfloat16)

        outputs = lax.map(one_batch, (tile_ids, weights, usable, offsets))
        current = jnp.transpose(outputs, (1, 0, 2, 3)).reshape(total_rows, NBLK * BLK)
    return current
```

```python
import functools

import jax
import jax.numpy as jnp
from jax import lax
from jax.experimental import pallas as pl
from jax.experimental.pallas import tpu as pltpu
from jax.sharding import PartitionSpec as P


def pick_kernel(layer, owned, groups, table, heavy, live, state_ref, out_ref, kept_ref):
    step = pl.program_id(0)
    blocks = state_ref.shape[0]
    dests = out_ref.shape[0]

    @pl.when(step == 0)
    def _():
        def mask(i, carry):
            kept_ref[i] = jnp.where(live[layer, i] > 0, state_ref[i], jnp.zeros_like(state_ref[i]))
            return carry

        lax.fori_loop(0, blocks, mask, 0, unroll=8)

    def one_dest(d, carry):
        dest = step * dests + d
        first = (dest % groups) * blocks + (dest // groups) * owned
        for k in range(owned):
            out_ref[d, k] = kept_ref[table[layer, 0, first + k]]
        out_ref[d, owned] = kept_ref[table[layer, 1, first + heavy[dest, layer]]]
        return carry

    lax.fori_loop(0, dests, one_dest, 0)


def pick(layer, owned, groups, table, heavy, live, state):
    blocks, rows, side = state.shape
    devices = heavy.shape[0]
    steps = 4
    return pl.pallas_call(
        functools.partial(pick_kernel, layer, owned, groups),
        out_shape=jax.ShapeDtypeStruct((devices, owned + 1, rows, side), state.dtype),
        grid_spec=pltpu.PrefetchScalarGridSpec(
            num_scalar_prefetch=3,
            grid=(steps,),
            in_specs=[pl.BlockSpec((blocks, rows, side), lambda i, *_: (0, 0, 0))],
            out_specs=pl.BlockSpec(
                (devices // steps, owned + 1, rows, side), lambda i, *_: (i, 0, 0, 0)
            ),
            scratch_shapes=[pltpu.VMEM((blocks, rows, side), state.dtype)],
        ),
        name=f"pick_{layer}",
    )(table, heavy, live, state)


def matmul_kernel(
    layer, counts, x_ref, rest_ref, w_ref, w_any, bias_ref, out_ref, acc_ref, wrest_ref, sem
):
    step = pl.program_id(0)
    across, groups, chunk, rows, side = x_ref.shape
    owned = counts.shape[1]
    total_rows = across * rows
    heavy = jnp.int32(0)
    for k in range(owned):
        heavy = jnp.where(counts[layer, k] > groups, k, heavy)
    copy = pltpu.make_async_copy(w_any.at[layer, 0, heavy, pl.ds(groups, groups)], wrest_ref, sem)

    @pl.when(step == 0)
    def _():
        copy.start()

    def gathered(ref, position, first, count):
        parts = []
        for g in range(groups):
            part = ref[:, g, position].reshape(total_rows, side)
            parts.append(jnp.where(first + g < count, part, jnp.zeros_like(part)))
        return jnp.concatenate(parts, axis=1)

    for c in range(chunk):
        k = step * chunk + c
        lhs = gathered(x_ref, c, 0, counts[layer, k])
        weight = w_ref[0, 0, c].reshape(groups * side, side)
        summed = jnp.dot(lhs, weight, preferred_element_type=jnp.float32)
        summed = summed + bias_ref[0, 0, pl.ds(k, 1), :]
        acc_ref[k] = summed
        out_ref[:, k] = (
            jnp.maximum(summed, 0.0).astype(out_ref.dtype).reshape(across, rows, side)
        )

    @pl.when(step == pl.num_programs(0) - 1)
    def _():
        copy.wait()
        lhs = gathered(rest_ref, 0, groups, counts[layer, heavy])
        weight = wrest_ref[...].reshape(groups * side, side)
        summed = acc_ref[heavy] + jnp.dot(lhs, weight, preferred_element_type=jnp.float32)
        out_ref[:, heavy] = (
            jnp.maximum(summed, 0.0).astype(out_ref.dtype).reshape(across, rows, side)
        )


def multiply(layer, counts, incoming, weight_tiles, bias_terms):
    across, groups, width, rows, side = incoming.shape
    owned = width - 1
    steps = 4 if owned % 4 == 0 else 1
    chunk = owned // steps
    return pl.pallas_call(
        functools.partial(matmul_kernel, layer),
        out_shape=jax.ShapeDtypeStruct((across, owned, rows, side), incoming.dtype),
        grid_spec=pltpu.PrefetchScalarGridSpec(
            num_scalar_prefetch=1,
            grid=(steps,),
            in_specs=[
                pl.BlockSpec((across, groups, chunk, rows, side), lambda i, *_: (0, 0, i, 0, 0)),
                pl.BlockSpec((across, groups, 1, rows, side), lambda i, *_: (0, 0, owned, 0, 0)),
                pl.BlockSpec(
                    (1, 1, chunk, groups, side, side), lambda i, *_: (layer, 0, i, 0, 0, 0)
                ),
                pl.BlockSpec(memory_space=pl.ANY),
                pl.BlockSpec((1, 1, owned, side), lambda i, *_: (layer, 0, 0, 0)),
            ],
            out_specs=pl.BlockSpec((across, owned, rows, side), lambda i, *_: (0, 0, 0, 0)),
            scratch_shapes=[
                pltpu.VMEM((owned, across * rows, side), jnp.float32),
                pltpu.VMEM((groups, side, side), weight_tiles.dtype),
                pltpu.SemaphoreType.DMA,
            ],
        ),
        name=f"multiply_{layer}",
    )(counts, incoming, incoming, weight_tiles, weight_tiles, bias_terms)


def local(activations, live_blocks, tile_index, tile_count, weight_tiles, bias_terms):
    across = lax.axis_size("gx")
    groups = lax.axis_size("gy")
    my_group = lax.axis_index("gy")
    layers = tile_index.shape[0]
    rows = activations.shape[0]
    side = weight_tiles.shape[-1]
    owned = weight_tiles.shape[2]
    blocks = activations.shape[1] // side
    devices = across * groups

    counts = tile_count[:, 0]
    spots = jnp.arange(owned, dtype=jnp.int32)
    heavy = jnp.sum(jnp.where(counts > groups, spots[None], 0), axis=1)
    heavy = jnp.pad(heavy, (0, side - layers))
    heavy_all = lax.all_to_all(
        jnp.broadcast_to(heavy, (devices, 1, side)), ("gx", "gy"), 0, 0, tiled=True
    )[:, 0, :layers]

    slots = jnp.transpose(tile_index, (0, 2, 1)).reshape(layers, -1, groups, tile_index.shape[1])
    table = lax.dynamic_index_in_dim(slots, my_group, 2, keepdims=False) - my_group * blocks
    live = live_blocks[:, 0]

    state = jnp.transpose(activations.reshape(rows, blocks, side), (1, 0, 2))
    for layer in range(layers):
        outgoing = pick(layer, owned, groups, table, heavy_all, live, state)
        incoming = lax.all_to_all(outgoing, ("gx", "gy"), 0, 0, tiled=True)
        incoming = incoming.reshape(across, groups, owned + 1, rows, side)
        result = multiply(layer, counts, incoming, weight_tiles, bias_terms)
        state = lax.all_to_all(result, "gx", 0, 0, tiled=True).reshape(blocks, rows, side)
    return jnp.transpose(state, (1, 0, 2)).reshape(rows, blocks * side)


def solution(mesh):
    placed = (
        P("gx", "gy"),
        P(None, "gx", "gy"),
        P(),
        P(None, "gy", "gx"),
        P(None, "gy", "gx", None, None, None),
        P(None, "gy", "gx", None),
    )
    return jax.shard_map(
        local, mesh=mesh, in_specs=placed, out_specs=P("gx", "gy"), check_vma=False
    )
```

```python
import functools

import jax
import jax.numpy as jnp
from jax import lax
from jax.experimental import pallas as pl
from jax.experimental.pallas import tpu as pltpu
from jax.sharding import Mesh, PartitionSpec as P

HALF, PAIR, REST, GROUP = "half", "pair", "rest", "gy"
ROWS_OVER = (HALF, PAIR, REST)
FETCH_OVER = (PAIR, REST, GROUP)


def pick_kernel(layer, owned, groups, where, table, heavy, live, *refs):
    *state_refs, out_ref, kept_ref = refs
    step = pl.program_id(0)
    blocks = kept_ref.shape[0]
    dests = out_ref.shape[0]
    half = where[0]

    @pl.when(step == 0)
    def _():
        if len(state_refs) == 2:
            own_ref, partner_ref = state_refs

            def mask(i, carry):
                own = own_ref[i]
                partner = partner_ref[i]
                kept_ref[i, half] = jnp.where(live[half, layer, i] > 0, own, jnp.zeros_like(own))
                kept_ref[i, 1 - half] = jnp.where(
                    live[1 - half, layer, i] > 0, partner, jnp.zeros_like(own)
                )
                return carry

            lax.fori_loop(0, blocks, mask, 0, unroll=8)
        else:
            (state_ref,) = state_refs
            batch = 8

            def mask(b, carry):
                pieces = []
                for i in range(batch):
                    for h in range(2):
                        tile = state_ref[b * batch + i, h]
                        alive = live[h, layer, b * batch + i] > 0
                        pieces.append(jnp.where(alive, tile, jnp.zeros_like(tile)))
                for i in range(batch):
                    for h in range(2):
                        kept_ref[b * batch + i, h] = pieces[2 * i + h]
                return carry

            lax.fori_loop(0, blocks // batch, mask, 0)

    def one_dest(d, carry):
        dest = step * dests + d
        owner = half * (dests * pl.num_programs(0) // groups) + dest // groups
        first = (dest % groups) * blocks + owner * owned
        spots = [table[layer, 0, first + k] for k in range(owned)]
        spots.append(table[layer, 1, first + heavy[dest, layer]])
        pieces = [kept_ref[spot] for spot in spots]
        for k, piece in enumerate(pieces):
            out_ref[d, k] = piece
        return carry

    lax.fori_loop(0, dests, one_dest, 0)


def pick(layer, owned, groups, where, table, heavy, live, states):
    blocks, (rows, side) = states[0].shape[0], states[0].shape[-2:]
    devices = heavy.shape[0]
    steps = 2
    return pl.pallas_call(
        functools.partial(pick_kernel, layer, owned, groups),
        out_shape=jax.ShapeDtypeStruct((devices, owned + 1, 2, rows, side), states[0].dtype),
        grid_spec=pltpu.PrefetchScalarGridSpec(
            num_scalar_prefetch=4,
            grid=(steps,),
            in_specs=[
                pl.BlockSpec(state.shape, lambda i, *_, n=state.ndim: (0,) * n) for state in states
            ],
            out_specs=pl.BlockSpec(
                (devices // steps, owned + 1, 2, rows, side), lambda i, *_: (i, 0, 0, 0, 0)
            ),
            scratch_shapes=[pltpu.VMEM((blocks, 2, rows, side), states[0].dtype)],
        ),
        name=f"pick_{layer}",
    )(where, table, heavy, live, *states)


def multiply_kernel(
    layer, last, where, counts, x_ref, rest_ref, w_ref, w_any, bias_ref, out_ref, acc_ref, wrest_ref, sem
):
    step = pl.program_id(0)
    across, groups, chunk, _, rows, side = x_ref.shape
    owned = counts.shape[1]
    total_rows = across * 2 * rows
    half = where[0]
    heavy = jnp.int32(0)
    for k in range(owned):
        heavy = jnp.where(counts[layer, k] > groups, k, heavy)
    copy = pltpu.make_async_copy(w_any.at[layer, 0, heavy, pl.ds(groups, groups)], wrest_ref, sem)

    @pl.when(step == 0)
    def _():
        copy.start()

    def gathered(ref, position, first, count):
        parts = []
        for g in range(groups):
            part = ref[:, g, position].reshape(total_rows, side)
            parts.append(jnp.where(first + g < count, part, jnp.zeros_like(part)))
        return jnp.concatenate(parts, axis=1)

    def write(k, summed):
        value = jnp.maximum(summed, 0.0).astype(out_ref.dtype)
        value = value.reshape(2, across // 2, 2, rows, side)
        if last:
            low, high = value[:, :, 0], value[:, :, 1]
            near = jnp.where(half == 0, low, high)
            far = jnp.where(half == 0, high, low)
        else:
            near = far = value
        out_ref[half, :, :, k] = near
        out_ref[1 - half, 0, :, k] = far[1]
        out_ref[1 - half, 1, :, k] = far[0]

    for c in range(chunk):
        k = step * chunk + c
        lhs = gathered(x_ref, c, 0, counts[layer, k])
        weight = w_ref[0, 0, c].reshape(groups * side, side)
        summed = jnp.dot(lhs, weight, preferred_element_type=jnp.float32)
        summed = summed + bias_ref[0, 0, pl.ds(k, 1), :]
        acc_ref[k] = summed
        write(k, summed)

    @pl.when(step == pl.num_programs(0) - 1)
    def _():
        copy.wait()
        lhs = gathered(rest_ref, 0, groups, counts[layer, heavy])
        weight = wrest_ref[...].reshape(groups * side, side)
        write(heavy, acc_ref[heavy] + jnp.dot(lhs, weight, preferred_element_type=jnp.float32))


def multiply(layer, last, where, counts, incoming, weight_tiles, bias_terms):
    across, groups, width, _, rows, side = incoming.shape
    owned = width - 1
    steps = 4 if owned % 4 == 0 else 1
    chunk = owned // steps
    out = (2, 2, across // 2, owned) + (() if last else (2,)) + (rows, side)
    return pl.pallas_call(
        functools.partial(multiply_kernel, layer, last),
        out_shape=jax.ShapeDtypeStruct(out, incoming.dtype),
        grid_spec=pltpu.PrefetchScalarGridSpec(
            num_scalar_prefetch=2,
            grid=(steps,),
            in_specs=[
                pl.BlockSpec(
                    (across, groups, chunk, 2, rows, side), lambda i, *_: (0, 0, i, 0, 0, 0)
                ),
                pl.BlockSpec(
                    (across, groups, 1, 2, rows, side), lambda i, *_: (0, 0, owned, 0, 0, 0)
                ),
                pl.BlockSpec(
                    (1, 1, chunk, groups, side, side), lambda i, *_: (layer, 0, i, 0, 0, 0)
                ),
                pl.BlockSpec(memory_space=pl.ANY),
                pl.BlockSpec((1, 1, owned, side), lambda i, *_: (layer, 0, 0, 0)),
            ],
            out_specs=pl.BlockSpec(out, lambda i, *_: (0,) * len(out)),
            scratch_shapes=[
                pltpu.VMEM((owned, across * 2 * rows, side), jnp.float32),
                pltpu.VMEM((groups, side, side), weight_tiles.dtype),
                pltpu.SemaphoreType.DMA,
            ],
        ),
        name=f"multiply_{layer}",
    )(where, counts, incoming, incoming, weight_tiles, weight_tiles, bias_terms)


def local(activations, live_blocks, tile_index, tile_count, weight_tiles, bias_terms):
    rest = lax.axis_size(REST)
    groups = lax.axis_size(GROUP)
    my_group = lax.axis_index(GROUP)
    my_half = lax.axis_index(HALF)
    layers = tile_index.shape[0]
    rows = activations.shape[0]
    side = weight_tiles.shape[-1]
    owned = weight_tiles.shape[2]
    blocks = activations.shape[1] // side
    devices = 2 * rest * groups
    partners = [
        ((h * 2 + p) * rest + r, ((1 - h) * 2 + 1 - p) * rest + r)
        for h in range(2)
        for p in range(2)
        for r in range(rest)
    ]

    own = jnp.transpose(activations.reshape(rows, blocks, side), (1, 0, 2))
    partner = lax.ppermute(own, ROWS_OVER, partners)
    live_own = live_blocks[:, 0]
    live_partner = lax.ppermute(live_own, ROWS_OVER, partners)
    live = jnp.where(
        my_half == 0, jnp.stack([live_own, live_partner]), jnp.stack([live_partner, live_own])
    )
    where = my_half.reshape(1)

    counts = tile_count[:, 0]
    spots = jnp.arange(owned, dtype=jnp.int32)
    heavy = jnp.sum(jnp.where(counts > groups, spots[None], 0), axis=1)
    heavy = jnp.pad(heavy, (0, side - layers))
    heavy_all = lax.all_to_all(
        jnp.broadcast_to(heavy, (devices, 1, side)), FETCH_OVER, 0, 0, tiled=True
    )[:, 0, :layers]

    slots = jnp.transpose(tile_index, (0, 2, 1)).reshape(layers, -1, groups, tile_index.shape[1])
    table = lax.dynamic_index_in_dim(slots, my_group, 2, keepdims=False) - my_group * blocks

    states = [own, partner]
    for layer in range(layers):
        last = layer == layers - 1
        outgoing = pick(layer, owned, groups, where, table, heavy_all, live, states)
        incoming = lax.all_to_all(outgoing, FETCH_OVER, 0, 0, tiled=True)
        incoming = incoming.reshape(2 * rest, groups, owned + 1, 2, rows, side)
        result = multiply(layer, last, where, counts, incoming, weight_tiles, bias_terms)
        result = result.reshape((4 * rest,) + result.shape[3:])
        returned = lax.all_to_all(result, ROWS_OVER, 0, 0, tiled=True)
        states = [returned.reshape((blocks,) + returned.shape[2:])]
    return jnp.transpose(states[0], (1, 0, 2)).reshape(rows, blocks * side)


def solution(mesh):
    across, groups = mesh.shape["gx"], mesh.shape["gy"]
    split = Mesh(mesh.devices.reshape(2, 2, across // 4, groups), (HALF, PAIR, REST, GROUP))
    placed = (
        P(ROWS_OVER, GROUP),
        P(None, ROWS_OVER, GROUP),
        P(),
        P(None, GROUP, ROWS_OVER),
        P(None, GROUP, ROWS_OVER, None, None, None),
        P(None, GROUP, ROWS_OVER, None),
    )
    return jax.shard_map(
        local, mesh=split, in_specs=placed, out_specs=P(ROWS_OVER, GROUP), check_vma=False
    )
```

```python
import functools

import jax
import jax.numpy as jnp
from jax import lax
from jax.experimental import pallas as pl
from jax.experimental.pallas import tpu as pltpu
from jax.sharding import Mesh, PartitionSpec as P

HALF, PAIR, REST, GROUP = "half", "pair", "rest", "gy"
ROWS_OVER = (HALF, PAIR, REST)
FETCH_OVER = (PAIR, REST, GROUP)


def pick_kernel(
    layer, layers, owned, groups, where, table, heavy, live_own, live_partner, *refs
):
    *state_refs, out_ref, kept_ref = refs
    step = pl.program_id(0)
    blocks = kept_ref.shape[0]
    dests = out_ref.shape[0]
    half = where[0]
    batch = 8

    def masked(alive, tile):
        return jnp.where(alive > 0, tile, jnp.zeros_like(tile))

    @pl.when(step == 0)
    def _():
        def mask(b, carry):
            first = b * batch
            own, partner = [], []
            for i in range(batch):
                if len(state_refs) == 2:
                    mine, other = state_refs[0][first + i], state_refs[1][first + i]
                else:
                    mine = state_refs[0][first + i, half]
                    other = state_refs[0][first + i, 1 - half]
                own.append(masked(live_own[layer * blocks + first + i], mine))
                partner.append(masked(live_partner[layer * blocks + first + i], other))
            for i in range(batch):
                kept_ref[first + i, half] = own[i]
                kept_ref[first + i, 1 - half] = partner[i]
            return carry

        lax.fori_loop(0, blocks // batch, mask, 0)

    across = dests * pl.num_programs(0) // groups
    slots = table.shape[0] // (2 * layers)

    def one_owner(o, carry):
        owner = step * (dests // groups) + o
        for g in range(groups):
            first = 2 * layer * slots + g * blocks + (half * across + owner) * owned
            spots = [table[first + k] for k in range(owned)]
            spots.append(table[first + slots + heavy[owner * groups + g, layer]])
            for k, spot in enumerate(spots):
                out_ref[o * groups + g, k] = kept_ref[spot]
        return carry

    lax.fori_loop(0, dests // groups, one_owner, 0)


def pick(layer, layers, owned, groups, where, table, heavy, live_own, live_partner, states):
    blocks, (rows, side) = states[0].shape[0], states[0].shape[-2:]
    devices = heavy.shape[0]
    steps = 2
    return pl.pallas_call(
        functools.partial(pick_kernel, layer, layers, owned, groups),
        out_shape=jax.ShapeDtypeStruct((devices, owned + 1, 2, rows, side), states[0].dtype),
        grid_spec=pltpu.PrefetchScalarGridSpec(
            num_scalar_prefetch=5,
            grid=(steps,),
            in_specs=[
                pl.BlockSpec(state.shape, lambda i, *_, n=state.ndim: (0,) * n) for state in states
            ],
            out_specs=pl.BlockSpec(
                (devices // steps, owned + 1, 2, rows, side), lambda i, *_: (i, 0, 0, 0, 0)
            ),
            scratch_shapes=[pltpu.VMEM((blocks, 2, rows, side), states[0].dtype)],
        ),
        compiler_params=pltpu.CompilerParams(vmem_limit_bytes=6 << 20),
        name=f"pick_{layer}",
    )(where, table, heavy, live_own, live_partner, *states)


def multiply_kernel(
    layer, last, where, counts, x_ref, rest_ref, w_hbm, bias_ref, out_ref, acc_ref, w_ref, wrest_ref, sems
):
    step = pl.program_id(0)
    steps = w_ref.shape[0]
    across, groups, chunk, _, rows, side = x_ref.shape
    owned = counts.shape[1]
    total_rows = across * 2 * rows
    half = where[0]
    heavy = jnp.int32(0)
    for k in range(owned):
        heavy = jnp.where(counts[layer, k] > groups, k, heavy)

    def fetch(i):
        return pltpu.make_async_copy(
            w_hbm.at[layer, 0, pl.ds(i * chunk, chunk), pl.ds(0, groups)], w_ref.at[i], sems.at[i]
        )

    fetch_rest = pltpu.make_async_copy(
        w_hbm.at[layer, 0, heavy, pl.ds(groups, groups)], wrest_ref, sems.at[steps]
    )

    @pl.when(step == 0)
    def _():
        for i in range(steps):
            fetch(i).start()
        fetch_rest.start()

    def gathered(ref, position, first, count):
        parts = []
        for g in range(groups):
            part = ref[:, g, position].reshape(total_rows, side)
            parts.append(jnp.where(first + g < count, part, jnp.zeros_like(part)))
        return jnp.concatenate(parts, axis=1)

    def write(k, summed):
        value = jnp.maximum(summed, 0.0).astype(out_ref.dtype)
        value = value.reshape(2, across // 2, 2, rows, side)
        if last:
            low, high = value[:, :, 0], value[:, :, 1]
            near = jnp.where(half == 0, low, high)
            far = jnp.where(half == 0, high, low)
        else:
            near = far = value
        out_ref[half, :, :, k] = near
        out_ref[1 - half, 0, :, k] = far[1]
        out_ref[1 - half, 1, :, k] = far[0]

    fetch(step).wait()
    for c in range(chunk):
        k = step * chunk + c
        lhs = gathered(x_ref, c, 0, counts[layer, k])
        weight = w_ref[step, c].reshape(groups * side, side)
        summed = jnp.dot(lhs, weight, preferred_element_type=jnp.float32)
        summed = summed + bias_ref[0, 0, pl.ds(k, 1), :]
        acc_ref[k] = summed
        write(k, summed)

    @pl.when(step == steps - 1)
    def _():
        fetch_rest.wait()
        lhs = gathered(rest_ref, 0, groups, counts[layer, heavy])
        weight = wrest_ref[...].reshape(groups * side, side)
        write(heavy, acc_ref[heavy] + jnp.dot(lhs, weight, preferred_element_type=jnp.float32))


def multiply(layer, last, where, counts, incoming, weight_tiles, bias_terms):
    across, groups, width, _, rows, side = incoming.shape
    owned = width - 1
    steps = 4 if owned % 4 == 0 else 1
    chunk = owned // steps
    out = (2, 2, across // 2, owned) + (() if last else (2,)) + (rows, side)
    return pl.pallas_call(
        functools.partial(multiply_kernel, layer, last),
        out_shape=jax.ShapeDtypeStruct(out, incoming.dtype),
        grid_spec=pltpu.PrefetchScalarGridSpec(
            num_scalar_prefetch=2,
            grid=(steps,),
            in_specs=[
                pl.BlockSpec(
                    (across, groups, chunk, 2, rows, side), lambda i, *_: (0, 0, i, 0, 0, 0)
                ),
                pl.BlockSpec(
                    (across, groups, 1, 2, rows, side), lambda i, *_: (0, 0, owned, 0, 0, 0)
                ),
                pl.BlockSpec(memory_space=pl.ANY),
                pl.BlockSpec((1, 1, owned, side), lambda i, *_: (layer, 0, 0, 0)),
            ],
            out_specs=pl.BlockSpec(out, lambda i, *_: (0,) * len(out)),
            scratch_shapes=[
                pltpu.VMEM((owned, across * 2 * rows, side), jnp.float32),
                pltpu.VMEM((steps, chunk, groups, side, side), weight_tiles.dtype),
                pltpu.VMEM((groups, side, side), weight_tiles.dtype),
                pltpu.SemaphoreType.DMA((steps + 1,)),
            ],
        ),
        compiler_params=pltpu.CompilerParams(vmem_limit_bytes=50 << 20),
        name=f"multiply_{layer}",
    )(where, counts, incoming, incoming, weight_tiles, bias_terms)


def local(activations, live_blocks, tile_index, tile_count, weight_tiles, bias_terms):
    rest = lax.axis_size(REST)
    groups = lax.axis_size(GROUP)
    my_group = lax.axis_index(GROUP)
    my_half = lax.axis_index(HALF)
    layers = tile_index.shape[0]
    rows = activations.shape[0]
    side = weight_tiles.shape[-1]
    owned = weight_tiles.shape[2]
    blocks = activations.shape[1] // side
    devices = 2 * rest * groups
    partners = [
        ((h * 2 + p) * rest + r, ((1 - h) * 2 + 1 - p) * rest + r)
        for h in range(2)
        for p in range(2)
        for r in range(rest)
    ]

    own = jnp.transpose(activations.reshape(rows, blocks, side), (1, 0, 2))
    partner = lax.ppermute(own, ROWS_OVER, partners)
    live_own = live_blocks[:, 0].reshape(-1)
    live_partner = lax.ppermute(live_blocks[:, 0], ROWS_OVER, partners).reshape(-1)
    where = my_half.reshape(1)

    counts = tile_count[:, 0]
    spots = jnp.arange(owned, dtype=jnp.int32)
    heavy = jnp.sum(jnp.where(counts > groups, spots[None], 0), axis=1)
    heavy = jnp.pad(heavy, (0, side - layers))
    heavy_all = lax.all_to_all(
        jnp.broadcast_to(heavy, (devices, 1, side)), FETCH_OVER, 0, 0, tiled=True
    )[:, 0, :layers]

    slots = jnp.transpose(tile_index, (0, 2, 1)).reshape(layers, -1, groups, tile_index.shape[1])
    table = lax.dynamic_index_in_dim(slots, my_group, 2, keepdims=False) - my_group * blocks
    table = table.reshape(-1)

    states = [own, partner]
    for layer in range(layers):
        last = layer == layers - 1
        outgoing = pick(
            layer, layers, owned, groups, where, table, heavy_all, live_own, live_partner, states
        )
        incoming = lax.all_to_all(outgoing, FETCH_OVER, 0, 0, tiled=True)
        incoming = incoming.reshape(2 * rest, groups, owned + 1, 2, rows, side)
        result = multiply(layer, last, where, counts, incoming, weight_tiles, bias_terms)
        result = result.reshape((4 * rest,) + result.shape[3:])
        returned = lax.all_to_all(result, ROWS_OVER, 0, 0, tiled=True)
        states = [returned.reshape((blocks,) + returned.shape[2:])]
    return jnp.transpose(states[0], (1, 0, 2)).reshape(rows, blocks * side)


def solution(mesh):
    across, groups = mesh.shape["gx"], mesh.shape["gy"]
    split = Mesh(mesh.devices.reshape(2, 2, across // 4, groups), (HALF, PAIR, REST, GROUP))
    placed = (
        P(ROWS_OVER, GROUP),
        P(None, ROWS_OVER, GROUP),
        P(),
        P(None, GROUP, ROWS_OVER),
        P(None, GROUP, ROWS_OVER, None, None, None),
        P(None, GROUP, ROWS_OVER, None),
    )
    return jax.shard_map(
        local, mesh=split, in_specs=placed, out_specs=P(ROWS_OVER, GROUP), check_vma=False
    )
```

```python
import functools

import jax
import jax.numpy as jnp
from jax import lax
from jax.experimental import pallas as pl
from jax.experimental.pallas import tpu as pltpu
from jax.sharding import Mesh, PartitionSpec as P

HALF, PAIR, REST, GROUP = "half", "pair", "rest", "gy"
ROWS_OVER = (HALF, PAIR, REST)
FETCH_OVER = (PAIR, REST, GROUP)


def masked(alive, tile):
    return jnp.where(alive > 0, tile, jnp.zeros_like(tile))


def prepare_kernel(groups, live, counts, rows_ref, live_ref, sent_ref, heavy_ref):
    layers, blocks = live_ref.shape
    tile = sent_ref.shape[1:]
    batch = 8

    def mask(b, carry):
        first = b * batch
        kept = [masked(live[first + i], rows_ref[first + i]) for i in range(batch)]
        for i in range(batch):
            sent_ref[first + i] = kept[i]
        return carry

    lax.fori_loop(0, blocks // batch, mask, 0)
    masks = live_ref[...].astype(jnp.float32)
    masks = jnp.concatenate([masks, jnp.zeros((tile[0] - layers, tile[1]), jnp.float32)], axis=0)
    sent_ref[blocks] = masks.astype(sent_ref.dtype)

    lane = lax.broadcasted_iota(jnp.int32, heavy_ref.shape[1:], 1)
    found = jnp.zeros_like(lane)
    for layer in range(layers):
        found = jnp.where(lane == layer, heavy_of(counts, layer, groups), found)
    heavy_ref[...] = jnp.broadcast_to(found[None], heavy_ref.shape)


def heavy_of(counts, layer, groups):
    heavy = jnp.int32(0)
    for k in range(counts.shape[1]):
        heavy = jnp.where(counts[layer, k] > groups, k, heavy)
    return heavy


def prepare(groups, devices, live, counts, own):
    blocks, rows, side = own.shape
    return pl.pallas_call(
        functools.partial(prepare_kernel, groups),
        out_shape=(
            jax.ShapeDtypeStruct((blocks + 1, rows, side), own.dtype),
            jax.ShapeDtypeStruct((devices, 1, side), jnp.int32),
        ),
        grid_spec=pltpu.PrefetchScalarGridSpec(
            num_scalar_prefetch=2,
            grid=(1,),
            in_specs=[
                pl.BlockSpec(own.shape, lambda i, *_: (0, 0, 0)),
                pl.BlockSpec(live.shape, lambda i, *_: (0, 0)),
            ],
            out_specs=(
                pl.BlockSpec((blocks + 1, rows, side), lambda i, *_: (0, 0, 0)),
                pl.BlockSpec((devices, 1, side), lambda i, *_: (0, 0, 0)),
            ),
        ),
        compiler_params=pltpu.CompilerParams(vmem_limit_bytes=6 << 20),
        name="prepare",
    )(*(pltpu.with_memory_space_constraint(x, pltpu.HBM) for x in (live.reshape(-1), counts, own, live)))


def pick_kernel(layer, layers, owned, groups, where, table, heavy, *refs):
    step = pl.program_id(0)
    half = where[0]
    if layer == 0:
        own_ref, partner_ref, out_ref, masks_ref = refs
        blocks = own_ref.shape[0] - 1

        @pl.when(step == 0)
        def _():
            masks = partner_ref[blocks].astype(jnp.float32).astype(jnp.int32)
            for i in range(layers):
                masks_ref[i] = masks[i : i + 1]

    else:
        live_own, live_partner, state_ref, out_ref, kept_ref = refs
        blocks = kept_ref.shape[0]
        batch = 8

        @pl.when(step == 0)
        def _():
            def mask(b, carry):
                first = b * batch
                kept = []
                for i in range(batch):
                    spot = layer * blocks + first + i
                    kept.append(masked(live_own[spot], state_ref[first + i, half]))
                    kept.append(masked(live_partner[spot], state_ref[first + i, 1 - half]))
                for i in range(batch):
                    kept_ref[first + i, half] = kept[2 * i]
                    kept_ref[first + i, 1 - half] = kept[2 * i + 1]
                return carry

            lax.fori_loop(0, blocks // batch, mask, 0)

    dests = out_ref.shape[0]
    across = dests * pl.num_programs(0) // groups
    slots = table.shape[0] // (2 * layers)

    def one_owner(o, carry):
        owner = step * (dests // groups) + o
        for g in range(groups):
            first = 2 * layer * slots + g * blocks + (half * across + owner) * owned
            spots = [table[first + k] for k in range(owned)]
            spots.append(table[first + slots + heavy[owner * groups + g, layer]])
            for k, spot in enumerate(spots):
                if layer == 0:
                    out_ref[o * groups + g, k, half] = own_ref[spot]
                    out_ref[o * groups + g, k, 1 - half] = partner_ref[spot]
                else:
                    out_ref[o * groups + g, k] = kept_ref[spot]
        return carry

    lax.fori_loop(0, dests // groups, one_owner, 0)


def pick(layer, layers, owned, groups, tables, states):
    blocks, (rows, side) = states[0].shape[0], states[0].shape[-2:]
    devices = tables[2].shape[0]
    steps = 2
    kept = [] if layer == 0 else [pltpu.VMEM((blocks, 2, rows, side), states[0].dtype)]
    out_shape = [jax.ShapeDtypeStruct((devices, owned + 1, 2, rows, side), states[0].dtype)]
    out_specs = [
        pl.BlockSpec((devices // steps, owned + 1, 2, rows, side), lambda i, *_: (i, 0, 0, 0, 0))
    ]
    if layer == 0:
        out_shape.append(jax.ShapeDtypeStruct((layers, 1, side), jnp.int32))
        out_specs.append(pl.BlockSpec((layers, 1, side), lambda i, *_: (0, 0, 0)))
    return pl.pallas_call(
        functools.partial(pick_kernel, layer, layers, owned, groups),
        out_shape=out_shape,
        grid_spec=pltpu.PrefetchScalarGridSpec(
            num_scalar_prefetch=len(tables),
            grid=(steps,),
            in_specs=[
                pl.BlockSpec(state.shape, lambda i, *_, n=state.ndim: (0,) * n) for state in states
            ],
            out_specs=out_specs,
            scratch_shapes=kept,
        ),
        compiler_params=pltpu.CompilerParams(vmem_limit_bytes=6 << 20),
        name=f"pick_{layer}",
    )(*tables, *states)


def multiply_kernel(
    layer, last, where, counts, x_ref, w_hbm, bias_ref, out_ref, acc_ref, w_ref, wrest_ref, sems
):
    step = pl.program_id(0)
    steps, chunk = w_ref.shape[:2]
    across, groups, _, _, rows, side = x_ref.shape
    owned = counts.shape[1]
    total_rows = across * 2 * rows
    half = where[0]
    heavy = heavy_of(counts, layer, groups)

    def fetch(i):
        return pltpu.make_async_copy(
            w_hbm.at[layer, 0, pl.ds(i * chunk, chunk), pl.ds(0, groups)], w_ref.at[i], sems.at[i]
        )

    fetch_rest = pltpu.make_async_copy(
        w_hbm.at[layer, 0, heavy, pl.ds(groups, groups)], wrest_ref, sems.at[steps]
    )

    @pl.when(step == 0)
    def _():
        for i in range(steps):
            fetch(i).start()
        fetch_rest.start()

    def gathered(position, first, count):
        parts = []
        for g in range(groups):
            part = x_ref[:, g, position].reshape(total_rows, side)
            parts.append(jnp.where(first + g < count, part, jnp.zeros_like(part)))
        return jnp.concatenate(parts, axis=1)

    def write(k, summed):
        value = jnp.maximum(summed, 0.0).astype(out_ref.dtype)
        value = value.reshape(2, across // 2, 2, rows, side)
        if last:
            low, high = value[:, :, 0], value[:, :, 1]
            near = jnp.where(half == 0, low, high)
            far = jnp.where(half == 0, high, low)
        else:
            near = far = value
        out_ref[half, :, :, k] = near
        out_ref[1 - half, 0, :, k] = far[1]
        out_ref[1 - half, 1, :, k] = far[0]

    fetch(step).wait()
    for c in range(chunk):
        k = step * chunk + c
        lhs = gathered(k, 0, counts[layer, k])
        weight = w_ref[step, c].reshape(groups * side, side)
        summed = jnp.dot(lhs, weight, preferred_element_type=jnp.float32)
        summed = summed + bias_ref[0, 0, pl.ds(k, 1), :]
        acc_ref[k] = summed
        write(k, summed)

    @pl.when(step == steps - 1)
    def _():
        fetch_rest.wait()
        lhs = gathered(owned, groups, counts[layer, heavy])
        weight = wrest_ref[...].reshape(groups * side, side)
        write(heavy, acc_ref[heavy] + jnp.dot(lhs, weight, preferred_element_type=jnp.float32))


def multiply(layer, last, where, counts, incoming, weight_tiles, bias_terms):
    across, groups, width, _, rows, side = incoming.shape
    owned = width - 1
    steps = 4 if owned % 4 == 0 else 1
    chunk = owned // steps
    out = (2, 2, across // 2, owned) + (() if last else (2,)) + (rows, side)
    return pl.pallas_call(
        functools.partial(multiply_kernel, layer, last),
        out_shape=jax.ShapeDtypeStruct(out, incoming.dtype),
        grid_spec=pltpu.PrefetchScalarGridSpec(
            num_scalar_prefetch=2,
            grid=(steps,),
            in_specs=[
                pl.BlockSpec(incoming.shape, lambda i, *_: (0,) * incoming.ndim),
                pl.BlockSpec(memory_space=pl.ANY),
                pl.BlockSpec((1, 1, owned, side), lambda i, *_: (layer, 0, 0, 0)),
            ],
            out_specs=pl.BlockSpec(out, lambda i, *_: (0,) * len(out)),
            scratch_shapes=[
                pltpu.VMEM((owned, across * 2 * rows, side), jnp.float32),
                pltpu.VMEM((steps, chunk, groups, side, side), weight_tiles.dtype),
                pltpu.VMEM((groups, side, side), weight_tiles.dtype),
                pltpu.SemaphoreType.DMA((steps + 1,)),
            ],
        ),
        compiler_params=pltpu.CompilerParams(vmem_limit_bytes=50 << 20),
        name=f"multiply_{layer}",
    )(where, counts, incoming, weight_tiles, bias_terms)


def local(activations, live_blocks, tile_index, tile_count, weight_tiles, bias_terms):
    rest = lax.axis_size(REST)
    groups = lax.axis_size(GROUP)
    my_group = lax.axis_index(GROUP)
    my_half = lax.axis_index(HALF)
    layers = tile_index.shape[0]
    rows = activations.shape[0]
    side = weight_tiles.shape[-1]
    owned = weight_tiles.shape[2]
    blocks = activations.shape[1] // side
    devices = 2 * rest * groups
    partners = [
        ((h * 2 + p) * rest + r, ((1 - h) * 2 + 1 - p) * rest + r)
        for h in range(2)
        for p in range(2)
        for r in range(rest)
    ]

    counts = tile_count[:, 0]
    live = live_blocks[:, 0]
    rows_first = jnp.transpose(activations.reshape(rows, blocks, side), (1, 0, 2))
    own, heavy = prepare(groups, devices, live, counts, rows_first)
    partner = lax.ppermute(own, ROWS_OVER, partners)
    heavy = lax.all_to_all(heavy, FETCH_OVER, 0, 0, tiled=True)[:, 0, :layers]
    live_own = live.reshape(-1)
    where = my_half.reshape(1)

    slots = jnp.transpose(tile_index, (0, 2, 1)).reshape(layers, -1, groups, tile_index.shape[1])
    table = lax.dynamic_index_in_dim(slots, my_group, 2, keepdims=False) - my_group * blocks
    table = table.reshape(-1)

    for layer in range(layers):
        last = layer == layers - 1
        if layer == 0:
            tables = (where, table, heavy)
            outgoing, masks = pick(layer, layers, owned, groups, tables, (own, partner))
            live_partner = masks.reshape(-1)
        else:
            tables = (where, table, heavy, live_own, live_partner)
            (outgoing,) = pick(layer, layers, owned, groups, tables, (state,))
        incoming = lax.all_to_all(outgoing, FETCH_OVER, 0, 0, tiled=True)
        incoming = incoming.reshape(2 * rest, groups, owned + 1, 2, rows, side)
        result = multiply(layer, last, where, counts, incoming, weight_tiles, bias_terms)
        result = result.reshape((4 * rest,) + result.shape[3:])
        returned = lax.all_to_all(result, ROWS_OVER, 0, 0, tiled=True)
        state = returned.reshape((blocks,) + returned.shape[2:])
    return jnp.transpose(state, (1, 0, 2)).reshape(rows, blocks * side)


def solution(mesh):
    across, groups = mesh.shape["gx"], mesh.shape["gy"]
    split = Mesh(mesh.devices.reshape(2, 2, across // 4, groups), (HALF, PAIR, REST, GROUP))
    placed = (
        P(ROWS_OVER, GROUP),
        P(None, ROWS_OVER, GROUP),
        P(),
        P(None, GROUP, ROWS_OVER),
        P(None, GROUP, ROWS_OVER, None, None, None),
        P(None, GROUP, ROWS_OVER, None),
    )
    return jax.shard_map(
        local, mesh=split, in_specs=placed, out_specs=P(ROWS_OVER, GROUP), check_vma=False
    )
```

```python
import functools

import jax
import jax.numpy as jnp
from jax import lax
from jax.experimental import pallas as pl
from jax.experimental.pallas import tpu as pltpu
from jax.sharding import Mesh, PartitionSpec as P

HALF, PAIR, REST, GROUP = "half", "pair", "rest", "gy"
ROWS_OVER = (HALF, PAIR, REST)
FETCH_OVER = (PAIR, REST, GROUP)


def masked(alive, tile):
    return jnp.where(alive > 0, tile, jnp.zeros_like(tile))


def announce_kernel(layers, groups, counts, heavy_ref):
    lane = lax.broadcasted_iota(jnp.int32, heavy_ref.shape[1:], 1)
    found = jnp.zeros_like(lane)
    for layer in range(layers):
        found = jnp.where(lane == layer, heavy_of(counts, layer, groups), found)
    heavy_ref[...] = jnp.broadcast_to(found[None], heavy_ref.shape)


def heavy_of(counts, layer, groups):
    heavy = jnp.int32(0)
    for k in range(counts.shape[1]):
        heavy = jnp.where(counts[layer, k] > groups, k, heavy)
    return heavy


def announce(groups, devices, side, counts):
    return pl.pallas_call(
        functools.partial(announce_kernel, counts.shape[0], groups),
        out_shape=jax.ShapeDtypeStruct((devices, 1, side), jnp.int32),
        grid_spec=pltpu.PrefetchScalarGridSpec(
            num_scalar_prefetch=1,
            grid=(1,),
            in_specs=[],
            out_specs=pl.BlockSpec((devices, 1, side), lambda i, *_: (0, 0, 0)),
        ),
        compiler_params=pltpu.CompilerParams(vmem_limit_bytes=4 << 20),
        name="announce",
    )(counts)


def mask_kernel(live, rows_ref, own_ref):
    batch = 8

    def mask(b, carry):
        first = b * batch
        kept = [masked(live[first + i], rows_ref[first + i]) for i in range(batch)]
        for i in range(batch):
            own_ref[first + i] = kept[i]
        return carry

    lax.fori_loop(0, rows_ref.shape[0] // batch, mask, 0)


def mask(live, own):
    live, own = (pltpu.with_memory_space_constraint(x, pltpu.HBM) for x in (live, own))
    spec = pl.BlockSpec(own.shape, lambda i, *_: (0, 0, 0))
    return pl.pallas_call(
        mask_kernel,
        out_shape=jax.ShapeDtypeStruct(own.shape, own.dtype),
        grid_spec=pltpu.PrefetchScalarGridSpec(
            num_scalar_prefetch=1, grid=(1,), in_specs=[spec], out_specs=spec
        ),
        compiler_params=pltpu.CompilerParams(vmem_limit_bytes=4 << 20),
        name="mask",
    )(live, own)


def pick_kernel(layer, layers, owned, groups, where, table, heavy, counts, *refs):
    step = pl.program_id(0)
    half = where[0]
    batch = 8
    *live_refs, w_hbm, out_ref, used_ref, rest_ref, kept_ref, sems = refs
    blocks = kept_ref.shape[0]
    copies = (
        pltpu.make_async_copy(w_hbm.at[layer, 0, :, pl.ds(0, groups)], used_ref, sems.at[0]),
        pltpu.make_async_copy(
            w_hbm.at[layer, 0, heavy_of(counts, layer, groups), pl.ds(groups, groups)],
            rest_ref,
            sems.at[1],
        ),
    )

    @pl.when(step == 0)
    def _():
        for copy in copies:
            copy.start()

    @pl.when(step == 0)
    def _():
        def mask(b, carry):
            first = b * batch
            kept = []
            for i in range(batch):
                spot = layer * blocks + first + i
                if layer == 0:
                    live_partner, own_ref, partner_ref = live_refs
                    kept.append(own_ref[first + i])
                    kept.append(masked(live_partner[spot], partner_ref[first + i]))
                else:
                    live_own, live_partner, state_ref = live_refs
                    kept.append(masked(live_own[spot], state_ref[first + i, half]))
                    kept.append(masked(live_partner[spot], state_ref[first + i, 1 - half]))
            for i in range(batch):
                kept_ref[first + i, half] = kept[2 * i]
                kept_ref[first + i, 1 - half] = kept[2 * i + 1]
            return carry

        lax.fori_loop(0, blocks // batch, mask, 0)

    dests = out_ref.shape[0]
    across = dests * pl.num_programs(0) // groups
    slots = table.shape[0] // (2 * layers)

    def one_owner(o, carry):
        owner = step * (dests // groups) + o
        for g in range(groups):
            first = 2 * layer * slots + g * blocks + (half * across + owner) * owned
            spots = [table[first + k] for k in range(owned)]
            spots.append(table[first + slots + heavy[owner * groups + g, layer]])
            for k, spot in enumerate(spots):
                out_ref[o * groups + g, k] = kept_ref[spot]
        return carry

    lax.fori_loop(0, dests // groups, one_owner, 0)

    @pl.when(step == pl.num_programs(0) - 1)
    def _():
        for copy in copies:
            copy.wait()


def pick(layer, layers, owned, groups, tables, states, weight_tiles):
    blocks, (rows, side) = states[0].shape[0], states[0].shape[-2:]
    devices = tables[2].shape[0]
    steps = 2
    used = (owned, groups, side, side)
    rest = (groups, side, side)
    return pl.pallas_call(
        functools.partial(pick_kernel, layer, layers, owned, groups),
        out_shape=(
            jax.ShapeDtypeStruct((devices, owned + 1, 2, rows, side), states[0].dtype),
            jax.ShapeDtypeStruct(used, weight_tiles.dtype),
            jax.ShapeDtypeStruct(rest, weight_tiles.dtype),
        ),
        grid_spec=pltpu.PrefetchScalarGridSpec(
            num_scalar_prefetch=len(tables),
            grid=(steps,),
            in_specs=[
                pl.BlockSpec(state.shape, lambda i, *_, n=state.ndim: (0,) * n) for state in states
            ]
            + [pl.BlockSpec(memory_space=pl.ANY)],
            out_specs=(
                pl.BlockSpec(
                    (devices // steps, owned + 1, 2, rows, side), lambda i, *_: (i, 0, 0, 0, 0)
                ),
                pl.BlockSpec(used, lambda i, *_: (0, 0, 0, 0)),
                pl.BlockSpec(rest, lambda i, *_: (0, 0, 0)),
            ),
            scratch_shapes=[
                pltpu.VMEM((blocks, 2, rows, side), states[0].dtype),
                pltpu.SemaphoreType.DMA((2,)),
            ],
        ),
        compiler_params=pltpu.CompilerParams(vmem_limit_bytes=12 << 20),
        name=f"pick_{layer}",
    )(*tables, *states, pltpu.with_memory_space_constraint(weight_tiles, pltpu.HBM))


def multiply_kernel(layer, last, where, counts, x_ref, w_ref, wrest_ref, bias_ref, out_ref, acc_ref):
    step = pl.program_id(0)
    across, groups, _, _, rows, side = x_ref.shape
    owned = counts.shape[1]
    chunk = owned // pl.num_programs(0)
    total_rows = across * 2 * rows
    half = where[0]

    def gathered(position, first, count):
        parts = []
        for g in range(groups):
            part = x_ref[:, g, position].reshape(total_rows, side)
            parts.append(jnp.where(first + g < count, part, jnp.zeros_like(part)))
        return jnp.concatenate(parts, axis=1)

    def write(k, summed):
        value = jnp.maximum(summed, 0.0).astype(out_ref.dtype)
        value = value.reshape(2, across // 2, 2, rows, side)
        if last:
            low, high = value[:, :, 0], value[:, :, 1]
            near = jnp.where(half == 0, low, high)
            far = jnp.where(half == 0, high, low)
        else:
            near = far = value
        out_ref[half, :, :, k] = near
        out_ref[1 - half, 0, :, k] = far[1]
        out_ref[1 - half, 1, :, k] = far[0]

    for c in range(chunk):
        k = step * chunk + c
        lhs = gathered(k, 0, counts[layer, k])
        weight = w_ref[k].reshape(groups * side, side)
        summed = jnp.dot(lhs, weight, preferred_element_type=jnp.float32)
        summed = summed + bias_ref[0, 0, pl.ds(k, 1), :]
        acc_ref[k] = summed
        write(k, summed)

    @pl.when(step == pl.num_programs(0) - 1)
    def _():
        heavy = heavy_of(counts, layer, groups)
        lhs = gathered(owned, groups, counts[layer, heavy])
        weight = wrest_ref[...].reshape(groups * side, side)
        write(heavy, acc_ref[heavy] + jnp.dot(lhs, weight, preferred_element_type=jnp.float32))


def multiply(layer, last, where, counts, incoming, used, rest, bias_terms):
    across, groups, width, _, rows, side = incoming.shape
    owned = width - 1
    steps = 4 if owned % 4 == 0 else 1
    out = (2, 2, across // 2, owned) + (() if last else (2,)) + (rows, side)
    return pl.pallas_call(
        functools.partial(multiply_kernel, layer, last),
        out_shape=jax.ShapeDtypeStruct(out, incoming.dtype),
        grid_spec=pltpu.PrefetchScalarGridSpec(
            num_scalar_prefetch=2,
            grid=(steps,),
            in_specs=[
                pl.BlockSpec(incoming.shape, lambda i, *_: (0,) * incoming.ndim),
                pl.BlockSpec(used.shape, lambda i, *_: (0, 0, 0, 0)),
                pl.BlockSpec(rest.shape, lambda i, *_: (0, 0, 0)),
                pl.BlockSpec((1, 1, owned, side), lambda i, *_: (layer, 0, 0, 0)),
            ],
            out_specs=pl.BlockSpec(out, lambda i, *_: (0,) * len(out)),
            scratch_shapes=[pltpu.VMEM((owned, across * 2 * rows, side), jnp.float32)],
        ),
        compiler_params=pltpu.CompilerParams(vmem_limit_bytes=12 << 20),
        name=f"multiply_{layer}",
    )(where, counts, incoming, used, rest, bias_terms)


def local(activations, live_blocks, tile_index, tile_count, weight_tiles, bias_terms):
    rest = lax.axis_size(REST)
    groups = lax.axis_size(GROUP)
    my_group = lax.axis_index(GROUP)
    my_half = lax.axis_index(HALF)
    layers = tile_index.shape[0]
    rows = activations.shape[0]
    side = weight_tiles.shape[-1]
    owned = weight_tiles.shape[2]
    blocks = activations.shape[1] // side
    devices = 2 * rest * groups
    partners = [
        ((h * 2 + p) * rest + r, ((1 - h) * 2 + 1 - p) * rest + r)
        for h in range(2)
        for p in range(2)
        for r in range(rest)
    ]

    counts = tile_count[:, 0]
    live = live_blocks[:, 0]
    own = jnp.transpose(activations.reshape(rows, blocks, side), (1, 0, 2))
    partner = lax.ppermute(own, ROWS_OVER, partners)
    counts_hbm = pltpu.with_memory_space_constraint(counts, pltpu.HBM)
    heavy = announce(groups, devices, side, counts_hbm)
    heavy = lax.all_to_all(heavy, FETCH_OVER, 0, 0, tiled=True)[:, 0, :layers]
    live_own = live.reshape(-1)
    live_partner = lax.ppermute(live, ROWS_OVER, partners).reshape(-1)
    own = mask(live_own, own)
    where = my_half.reshape(1)

    slots = jnp.transpose(tile_index, (0, 2, 1)).reshape(layers, -1, groups, tile_index.shape[1])
    table = lax.dynamic_index_in_dim(slots, my_group, 2, keepdims=False) - my_group * blocks
    table = table.reshape(-1)

    for layer in range(layers):
        last = layer == layers - 1
        if layer == 0:
            tables, states = (where, table, heavy, counts_hbm, live_partner), (own, partner)
        else:
            tables, states = (where, table, heavy, counts, live_own, live_partner), (state,)
        outgoing, used, extra = pick(layer, layers, owned, groups, tables, states, weight_tiles)
        incoming = lax.all_to_all(outgoing, FETCH_OVER, 0, 0, tiled=True)
        incoming = incoming.reshape(2 * rest, groups, owned + 1, 2, rows, side)
        result = multiply(layer, last, where, counts, incoming, used, extra, bias_terms)
        result = result.reshape((4 * rest,) + result.shape[3:])
        returned = lax.all_to_all(result, ROWS_OVER, 0, 0, tiled=True)
        state = returned.reshape((blocks,) + returned.shape[2:])
    return jnp.transpose(state, (1, 0, 2)).reshape(rows, blocks * side)


def solution(mesh):
    across, groups = mesh.shape["gx"], mesh.shape["gy"]
    split = Mesh(mesh.devices.reshape(2, 2, across // 4, groups), (HALF, PAIR, REST, GROUP))
    placed = (
        P(ROWS_OVER, GROUP),
        P(None, ROWS_OVER, GROUP),
        P(),
        P(None, GROUP, ROWS_OVER),
        P(None, GROUP, ROWS_OVER, None, None, None),
        P(None, GROUP, ROWS_OVER, None),
    )
    return jax.shard_map(
        local, mesh=split, in_specs=placed, out_specs=P(ROWS_OVER, GROUP), check_vma=False
    )
```

```python
import functools

import jax
import jax.numpy as jnp
from jax import lax
from jax.experimental import pallas as pl
from jax.experimental.pallas import tpu as pltpu
from jax.sharding import Mesh, PartitionSpec as P

HALF, PAIR, REST, GROUP = "half", "pair", "rest", "gy"
ROWS_OVER = (HALF, PAIR, REST)
FETCH_OVER = (PAIR, REST, GROUP)


def masked(alive, tile):
    return jnp.where(alive > 0, tile, jnp.zeros_like(tile))


def announce_kernel(layers, groups, counts, heavy_ref):
    lane = lax.broadcasted_iota(jnp.int32, heavy_ref.shape[1:], 1)
    found = jnp.zeros_like(lane)
    for layer in range(layers):
        found = jnp.where(lane == layer, heavy_of(counts, layer, groups), found)
    heavy_ref[...] = jnp.broadcast_to(found[None], heavy_ref.shape)


def heavy_of(counts, layer, groups):
    heavy = jnp.int32(0)
    for k in range(counts.shape[1]):
        heavy = jnp.where(counts[layer, k] > groups, k, heavy)
    return heavy


def announce(groups, devices, side, counts):
    return pl.pallas_call(
        functools.partial(announce_kernel, counts.shape[0], groups),
        out_shape=jax.ShapeDtypeStruct((devices, 1, side), jnp.int32),
        grid_spec=pltpu.PrefetchScalarGridSpec(
            num_scalar_prefetch=1,
            grid=(1,),
            in_specs=[],
            out_specs=pl.BlockSpec((devices, 1, side), lambda i, *_: (0, 0, 0)),
        ),
        compiler_params=pltpu.CompilerParams(vmem_limit_bytes=4 << 20),
        name="announce",
    )(counts)


def mask_kernel(live, rows_ref, own_ref):
    batch = 8

    def mask(b, carry):
        first = b * batch
        kept = [masked(live[first + i], rows_ref[first + i]) for i in range(batch)]
        for i in range(batch):
            own_ref[first + i] = kept[i]
        return carry

    lax.fori_loop(0, rows_ref.shape[0] // batch, mask, 0)


def mask(live, own):
    live, own = (pltpu.with_memory_space_constraint(x, pltpu.HBM) for x in (live, own))
    spec = pl.BlockSpec(own.shape, lambda i, *_: (0, 0, 0))
    return pl.pallas_call(
        mask_kernel,
        out_shape=jax.ShapeDtypeStruct(own.shape, own.dtype),
        grid_spec=pltpu.PrefetchScalarGridSpec(
            num_scalar_prefetch=1, grid=(1,), in_specs=[spec], out_specs=spec
        ),
        compiler_params=pltpu.CompilerParams(vmem_limit_bytes=4 << 20),
        name="mask",
    )(live, own)


def pick_kernel(layer, owned, groups, where, heavy, *refs):
    half = where[0]
    batch = 8
    *live_refs, table, w_hbm, out_ref, used_ref, kept_ref, sem = refs
    blocks = kept_ref.shape[0]
    fetch = pltpu.make_async_copy(
        w_hbm.at[layer, 0, pl.ds(0, used_ref.shape[0]), pl.ds(0, groups)], used_ref, sem
    )
    fetch.start()

    def mask(b, carry):
        first = b * batch
        kept = []
        for i in range(batch):
            spot = layer * blocks + first + i
            if layer == 0:
                live_partner, own_ref, partner_ref = live_refs
                kept.append(own_ref[first + i])
                kept.append(masked(live_partner[spot], partner_ref[first + i]))
            else:
                live_own, live_partner, state_ref = live_refs
                kept.append(masked(live_own[spot], state_ref[first + i, half]))
                kept.append(masked(live_partner[spot], state_ref[first + i, 1 - half]))
        for i in range(batch):
            kept_ref[first + i, half] = kept[2 * i]
            kept_ref[first + i, 1 - half] = kept[2 * i + 1]
        return carry

    lax.fori_loop(0, blocks // batch, mask, 0)

    across = out_ref.shape[0] // groups
    slots = table.shape[0] // 2

    def one_owner(owner, carry):
        for g in range(groups):
            first = g * blocks + (half * across + owner) * owned
            spots = [table[first + k] for k in range(owned)]
            spots.append(table[first + slots + heavy[owner * groups + g, layer]])
            for k, spot in enumerate(spots):
                out_ref[owner * groups + g, k] = kept_ref[spot]
        return carry

    lax.fori_loop(0, across, one_owner, 0)
    fetch.wait()


def early(owned):
    return owned // 2 if owned % 2 == 0 else owned


def pick(layer, layers, owned, groups, table, scalars, states, weight_tiles):
    blocks, (rows, side) = states[0].shape[0], states[0].shape[-2:]
    devices = scalars[1].shape[0]
    shapes = ((devices, owned + 1, 2, rows, side), (early(owned), groups, side, side))
    return pl.pallas_call(
        functools.partial(pick_kernel, layer, owned, groups),
        out_shape=tuple(jax.ShapeDtypeStruct(shape, weight_tiles.dtype) for shape in shapes),
        grid_spec=pltpu.PrefetchScalarGridSpec(
            num_scalar_prefetch=len(scalars),
            grid=(1,),
            in_specs=[
                pl.BlockSpec(state.shape, lambda i, *_, n=state.ndim: (0,) * n) for state in states
            ]
            + [
                pl.BlockSpec(
                    (table.shape[0] // layers,), lambda i, *_: (layer,), memory_space=pltpu.SMEM
                ),
                pl.BlockSpec(memory_space=pl.ANY),
            ],
            out_specs=tuple(
                pl.BlockSpec(shape, lambda i, *_, n=len(shape): (0,) * n) for shape in shapes
            ),
            scratch_shapes=[
                pltpu.VMEM((blocks, 2, rows, side), states[0].dtype),
                pltpu.SemaphoreType.DMA,
            ],
        ),
        compiler_params=pltpu.CompilerParams(vmem_limit_bytes=12 << 20),
    )(*scalars, *states, table, pltpu.with_memory_space_constraint(weight_tiles, pltpu.HBM))


def multiply_kernel(
    layer, last, where, counts, x_ref, used_ref, w_hbm, bias_ref, out_ref, acc_ref, late_ref, rest_ref, sems
):
    step = pl.program_id(0)
    steps = pl.num_programs(0)
    across, groups, _, _, rows, side = x_ref.shape
    owned = counts.shape[1]
    chunk = used_ref.shape[0]
    total_rows = across * 2 * rows
    half = where[0]
    heavy = heavy_of(counts, layer, groups)
    fetches = [
        pltpu.make_async_copy(
            w_hbm.at[layer, 0, heavy, pl.ds(groups, groups)], rest_ref, sems.at[0]
        )
    ]
    if chunk < owned:
        fetches.append(
            pltpu.make_async_copy(
                w_hbm.at[layer, 0, pl.ds(chunk, chunk), pl.ds(0, groups)], late_ref, sems.at[1]
            )
        )

    @pl.when(step == 0)
    def _():
        for fetch in reversed(fetches):
            fetch.start()

    def gathered(position, first, count):
        parts = []
        for g in range(groups):
            part = x_ref[:, g, position].reshape(total_rows, side)
            parts.append(jnp.where(first + g < count, part, jnp.zeros_like(part)))
        return jnp.concatenate(parts, axis=1)

    def write(k, summed):
        value = jnp.maximum(summed, 0.0).astype(out_ref.dtype)
        value = value.reshape(2, across // 2, 2, rows, side)
        if last:
            low, high = value[:, :, 0], value[:, :, 1]
            near = jnp.where(half == 0, low, high)
            far = jnp.where(half == 0, high, low)
        else:
            near = far = value
        out_ref[half, :, :, k] = near
        out_ref[1 - half, 0, :, k] = far[1]
        out_ref[1 - half, 1, :, k] = far[0]

    def blocks_of(first, weights):
        for c in range(chunk):
            k = first + c
            weight = weights[c].reshape(groups * side, side)
            summed = jnp.dot(
                gathered(k, 0, counts[layer, k]), weight, preferred_element_type=jnp.float32
            )
            summed = summed + bias_ref[0, 0, k : k + 1, :]
            acc_ref[k] = summed
            write(k, summed)

    @pl.when(step == 0)
    def _():
        blocks_of(0, used_ref)

    @pl.when(step == steps - 1)
    def _():
        for fetch in fetches:
            fetch.wait()
        if chunk < owned:
            blocks_of(chunk, late_ref)
        lhs = gathered(owned, groups, counts[layer, heavy])
        weight = rest_ref[...].reshape(groups * side, side)
        write(heavy, acc_ref[heavy] + jnp.dot(lhs, weight, preferred_element_type=jnp.float32))


def multiply(layer, last, where, counts, incoming, used, weight_tiles, bias_terms):
    across, groups, width, _, rows, side = incoming.shape
    owned = width - 1
    out = (2, 2, across // 2, owned) + (() if last else (2,)) + (rows, side)
    return pl.pallas_call(
        functools.partial(multiply_kernel, layer, last),
        out_shape=jax.ShapeDtypeStruct(out, incoming.dtype),
        grid_spec=pltpu.PrefetchScalarGridSpec(
            num_scalar_prefetch=2,
            grid=(owned // used.shape[0],),
            in_specs=[
                pl.BlockSpec(incoming.shape, lambda i, *_: (0,) * incoming.ndim),
                pl.BlockSpec(used.shape, lambda i, *_: (0, 0, 0, 0)),
                pl.BlockSpec(memory_space=pl.ANY),
                pl.BlockSpec((1, 1, owned, side), lambda i, *_: (layer, 0, 0, 0)),
            ],
            out_specs=pl.BlockSpec(out, lambda i, *_: (0,) * len(out)),
            scratch_shapes=[
                pltpu.VMEM((owned, across * 2 * rows, side), jnp.float32),
                pltpu.VMEM(used.shape, used.dtype),
                pltpu.VMEM((groups, side, side), used.dtype),
                pltpu.SemaphoreType.DMA((2,)),
            ],
        ),
        compiler_params=pltpu.CompilerParams(vmem_limit_bytes=12 << 20),
    )(
        where,
        counts,
        incoming,
        used,
        pltpu.with_memory_space_constraint(weight_tiles, pltpu.HBM),
        bias_terms,
    )


def local(activations, live_blocks, tile_index, tile_count, weight_tiles, bias_terms):
    rest = lax.axis_size(REST)
    groups = lax.axis_size(GROUP)
    my_group = lax.axis_index(GROUP)
    my_half = lax.axis_index(HALF)
    layers = tile_index.shape[0]
    rows = activations.shape[0]
    side = weight_tiles.shape[-1]
    owned = weight_tiles.shape[2]
    blocks = activations.shape[1] // side
    devices = 2 * rest * groups
    partners = [
        ((h * 2 + p) * rest + r, ((1 - h) * 2 + 1 - p) * rest + r)
        for h in range(2)
        for p in range(2)
        for r in range(rest)
    ]

    counts = tile_count[:, 0]
    live = live_blocks[:, 0]
    own = jnp.transpose(activations.reshape(rows, blocks, side), (1, 0, 2))
    partner = lax.ppermute(own, ROWS_OVER, partners)
    counts_hbm = pltpu.with_memory_space_constraint(counts, pltpu.HBM)
    heavy = announce(groups, devices, side, counts_hbm)
    heavy = lax.all_to_all(heavy, FETCH_OVER, 0, 0, tiled=True)
    heavy = heavy[:, 0, :layers]
    live_own = live.reshape(-1)
    live_partner = lax.ppermute(live, ROWS_OVER, partners)
    live_partner = live_partner.reshape(-1)
    own = mask(live_own, own)
    where = my_half.reshape(1)

    slots = jnp.transpose(tile_index, (0, 2, 1)).reshape(layers, -1, groups, tile_index.shape[1])
    table = lax.dynamic_index_in_dim(slots, my_group, 2, keepdims=False) - my_group * blocks
    table = table.reshape(-1)

    for layer in range(layers):
        last = layer == layers - 1
        if layer == 0:
            scalars, states = (where, heavy, live_partner), (own, partner)
        else:
            scalars, states = (where, heavy, live_own, live_partner), (state,)
        outgoing, used = pick(
            layer, layers, owned, groups, table, scalars, states, weight_tiles
        )
        incoming = lax.all_to_all(outgoing, FETCH_OVER, 0, 0, tiled=True)
        incoming = incoming.reshape(2 * rest, groups, owned + 1, 2, rows, side)
        result = multiply(layer, last, where, counts, incoming, used, weight_tiles, bias_terms)
        result = result.reshape((4 * rest,) + result.shape[3:])
        returned = lax.all_to_all(result, ROWS_OVER, 0, 0, tiled=True)
        state = returned.reshape((blocks,) + returned.shape[2:])
    return jnp.transpose(state, (1, 0, 2)).reshape(rows, blocks * side)


def solution(mesh):
    across, groups = mesh.shape["gx"], mesh.shape["gy"]
    split = Mesh(mesh.devices.reshape(2, 2, across // 4, groups), (HALF, PAIR, REST, GROUP))
    placed = (
        P(ROWS_OVER, GROUP),
        P(None, ROWS_OVER, GROUP),
        P(),
        P(None, GROUP, ROWS_OVER),
        P(None, GROUP, ROWS_OVER, None, None, None),
        P(None, GROUP, ROWS_OVER, None),
    )
    return jax.shard_map(
        local, mesh=split, in_specs=placed, out_specs=P(ROWS_OVER, GROUP), check_vma=False
    )
```

```python
import functools

import jax
import jax.numpy as jnp
from jax import lax
from jax.experimental import pallas as pl
from jax.experimental.pallas import tpu as pltpu
from jax.sharding import Mesh, PartitionSpec as P

HALF, PAIR, REST, GROUP = "half", "pair", "rest", "gy"
ROWS_OVER = (HALF, PAIR, REST)
FETCH_OVER = (PAIR, REST, GROUP)


def masked(alive, tile):
    return jnp.where(alive > 0, tile, jnp.zeros_like(tile))


def announce_kernel(layers, groups, counts, heavy_ref):
    lane = lax.broadcasted_iota(jnp.int32, heavy_ref.shape[1:], 1)
    found = jnp.zeros_like(lane)
    for layer in range(layers):
        found = jnp.where(lane == layer, heavy_of(counts, layer, groups), found)
    heavy_ref[...] = jnp.broadcast_to(found[None], heavy_ref.shape)


def heavy_of(counts, layer, groups):
    heavy = jnp.int32(0)
    for k in range(counts.shape[1]):
        heavy = jnp.where(counts[layer, k] > groups, k, heavy)
    return heavy


def announce(groups, devices, side, counts):
    return pl.pallas_call(
        functools.partial(announce_kernel, counts.shape[0], groups),
        out_shape=jax.ShapeDtypeStruct((devices, 1, side), jnp.int32),
        grid_spec=pltpu.PrefetchScalarGridSpec(
            num_scalar_prefetch=1,
            grid=(1,),
            in_specs=[],
            out_specs=pl.BlockSpec((devices, 1, side), lambda i, *_: (0, 0, 0)),
        ),
        compiler_params=pltpu.CompilerParams(vmem_limit_bytes=4 << 20),
        name="announce",
    )(counts)


def mask_kernel(live, rows_ref, own_ref):
    batch = 8

    def mask(b, carry):
        first = b * batch
        kept = [masked(live[first + i], rows_ref[first + i]) for i in range(batch)]
        for i in range(batch):
            own_ref[first + i] = kept[i]
        return carry

    lax.fori_loop(0, rows_ref.shape[0] // batch, mask, 0)


def mask(live, own):
    live, own = (pltpu.with_memory_space_constraint(x, pltpu.HBM) for x in (live, own))
    spec = pl.BlockSpec(own.shape, lambda i, *_: (0, 0, 0))
    return pl.pallas_call(
        mask_kernel,
        out_shape=jax.ShapeDtypeStruct(own.shape, own.dtype),
        grid_spec=pltpu.PrefetchScalarGridSpec(
            num_scalar_prefetch=1, grid=(1,), in_specs=[spec], out_specs=spec
        ),
        compiler_params=pltpu.CompilerParams(vmem_limit_bytes=4 << 20),
        name="mask",
    )(live, own)


def pick_kernel(layer, owned, groups, where, heavy, *refs):
    half = where[0]
    batch = 8
    if layer == 0:
        counts, *live_refs, table, w_hbm, out_ref, used_ref, rest_ref, kept_ref, sems = refs
        extra = heavy_of(counts, layer, groups)
        fetches = (
            pltpu.make_async_copy(w_hbm.at[layer, 0, :, pl.ds(0, groups)], used_ref, sems.at[0]),
            pltpu.make_async_copy(
                w_hbm.at[layer, 0, extra, pl.ds(groups, groups)], rest_ref, sems.at[1]
            ),
        )
        for fetch in fetches:
            fetch.start()
    else:
        *live_refs, table, out_ref, kept_ref = refs
    blocks = kept_ref.shape[0]

    def mask(b, carry):
        first = b * batch
        kept = []
        for i in range(batch):
            spot = layer * blocks + first + i
            if layer == 0:
                live_partner, own_ref, partner_ref = live_refs
                kept.append(own_ref[first + i])
                kept.append(masked(live_partner[spot], partner_ref[first + i]))
            else:
                live_own, live_partner, state_ref = live_refs
                kept.append(masked(live_own[spot], state_ref[first + i, half]))
                kept.append(masked(live_partner[spot], state_ref[first + i, 1 - half]))
        for i in range(batch):
            kept_ref[first + i, half] = kept[2 * i]
            kept_ref[first + i, 1 - half] = kept[2 * i + 1]
        return carry

    lax.fori_loop(0, blocks // batch, mask, 0)

    across = out_ref.shape[0] // groups
    slots = table.shape[0] // 2

    def one_owner(owner, carry):
        for g in range(groups):
            first = g * blocks + (half * across + owner) * owned
            spots = [table[first + k] for k in range(owned)]
            spots.append(table[first + slots + heavy[owner * groups + g, layer]])
            for k, spot in enumerate(spots):
                out_ref[owner * groups + g, k] = kept_ref[spot]
        return carry

    lax.fori_loop(0, across, one_owner, 0)
    if layer == 0:
        for fetch in fetches:
            fetch.wait()


def whole(shape):
    return pl.BlockSpec(shape, lambda i, *_: (0,) * len(shape))


def pick(layer, layers, owned, groups, table, scalars, states, weight_tiles):
    blocks, (rows, side) = states[0].shape[0], states[0].shape[-2:]
    devices = scalars[1].shape[0]
    piece = pl.BlockSpec(
        (table.shape[0] // layers,), lambda i, *_: (layer,), memory_space=pltpu.SMEM
    )
    operands = [*states, table]
    in_specs = [whole(state.shape) for state in states] + [piece]
    shapes = [(devices, owned + 1, 2, rows, side)]
    scratch = [pltpu.VMEM((blocks, 2, rows, side), states[0].dtype)]
    if layer == 0:
        operands.append(pltpu.with_memory_space_constraint(weight_tiles, pltpu.HBM))
        in_specs.append(pl.BlockSpec(memory_space=pl.ANY))
        shapes += [(owned, groups, side, side), (groups, side, side)]
        scratch.append(pltpu.SemaphoreType.DMA((2,)))
    return pl.pallas_call(
        functools.partial(pick_kernel, layer, owned, groups),
        out_shape=[jax.ShapeDtypeStruct(shape, states[0].dtype) for shape in shapes],
        grid_spec=pltpu.PrefetchScalarGridSpec(
            num_scalar_prefetch=len(scalars),
            grid=(1,),
            in_specs=in_specs,
            out_specs=[whole(shape) for shape in shapes],
            scratch_shapes=scratch,
        ),
        compiler_params=pltpu.CompilerParams(vmem_limit_bytes=(12 if layer == 0 else 6) << 20),
    )(*scalars, *operands)


def multiply_kernel(layer, last, where, counts, x_ref, *refs):
    *w_refs, bias_ref, out_ref, acc_ref = refs
    across, groups, _, _, rows, side = x_ref.shape
    owned = counts.shape[1]
    total_rows = across * 2 * rows
    half = where[0]
    heavy = heavy_of(counts, layer, groups)

    def gathered(position, first, count):
        parts = []
        for g in range(groups):
            part = x_ref[:, g, position].reshape(total_rows, side)
            parts.append(jnp.where(first + g < count, part, jnp.zeros_like(part)))
        return jnp.concatenate(parts, axis=1)

    def write(k, summed):
        value = jnp.maximum(summed, 0.0).astype(out_ref.dtype)
        value = value.reshape(2, across // 2, 2, rows, side)
        if last:
            low, high = value[:, :, 0], value[:, :, 1]
            near = jnp.where(half == 0, low, high)
            far = jnp.where(half == 0, high, low)
        else:
            near = far = value
        out_ref[half, :, :, k] = near
        out_ref[1 - half, 0, :, k] = far[1]
        out_ref[1 - half, 1, :, k] = far[0]

    def product(position, first, count, weight):
        weight = weight.reshape(groups * side, side)
        lhs = gathered(position, first, count)
        return jnp.dot(lhs, weight, preferred_element_type=jnp.float32)

    for k in range(owned):
        weight = w_refs[0][k] if layer == 0 else w_refs[0][layer, 0, k, :groups]
        summed = product(k, 0, counts[layer, k], weight) + bias_ref[0, 0, k : k + 1, :]
        acc_ref[k] = summed
        write(k, summed)

    weight = w_refs[1][...] if layer == 0 else w_refs[0][layer, 0, heavy, groups:]
    write(heavy, acc_ref[heavy] + product(owned, groups, counts[layer, heavy], weight))


def multiply(layer, last, where, counts, incoming, weights, bias_terms):
    across, _, width, _, rows, side = incoming.shape
    owned = width - 1
    out = (2, 2, across // 2, owned) + (() if last else (2,)) + (rows, side)
    return pl.pallas_call(
        functools.partial(multiply_kernel, layer, last),
        out_shape=jax.ShapeDtypeStruct(out, incoming.dtype),
        grid_spec=pltpu.PrefetchScalarGridSpec(
            num_scalar_prefetch=2,
            grid=(1,),
            in_specs=[
                whole(incoming.shape),
                *(whole(weight.shape) for weight in weights),
                pl.BlockSpec((1, 1, owned, side), lambda i, *_: (layer, 0, 0, 0)),
            ],
            out_specs=whole(out),
            scratch_shapes=[pltpu.VMEM((owned, across * 2 * rows, side), jnp.float32)],
        ),
        compiler_params=pltpu.CompilerParams(vmem_limit_bytes=(12 if layer == 0 else 24) << 20),
    )(where, counts, incoming, *weights, bias_terms)


def local(activations, live_blocks, tile_index, tile_count, weight_tiles, bias_terms):
    rest = lax.axis_size(REST)
    groups = lax.axis_size(GROUP)
    my_group = lax.axis_index(GROUP)
    my_half = lax.axis_index(HALF)
    layers = tile_index.shape[0]
    rows = activations.shape[0]
    side = weight_tiles.shape[-1]
    owned = weight_tiles.shape[2]
    blocks = activations.shape[1] // side
    devices = 2 * rest * groups
    partners = [
        ((h * 2 + p) * rest + r, ((1 - h) * 2 + 1 - p) * rest + r)
        for h in range(2)
        for p in range(2)
        for r in range(rest)
    ]

    counts = tile_count[:, 0]
    live = live_blocks[:, 0]
    own = jnp.transpose(activations.reshape(rows, blocks, side), (1, 0, 2))
    partner = lax.ppermute(own, ROWS_OVER, partners)
    counts_hbm = pltpu.with_memory_space_constraint(counts, pltpu.HBM)
    heavy = announce(groups, devices, side, counts_hbm)
    heavy = lax.all_to_all(heavy, FETCH_OVER, 0, 0, tiled=True)
    heavy = heavy[:, 0, :layers]
    live_own = live.reshape(-1)
    live_partner = lax.ppermute(live, ROWS_OVER, partners)
    live_partner = live_partner.reshape(-1)
    own = mask(live_own, own)
    where = my_half.reshape(1)

    slots = jnp.transpose(tile_index, (0, 2, 1)).reshape(layers, -1, groups, tile_index.shape[1])
    table = lax.dynamic_index_in_dim(slots, my_group, 2, keepdims=False) - my_group * blocks
    table = table.reshape(-1)

    for layer in range(layers):
        last = layer == layers - 1
        if layer == 0:
            scalars, states = (where, heavy, counts_hbm, live_partner), (own, partner)
        else:
            scalars, states = (where, heavy, live_own, live_partner), (state,)
        outgoing, *weights = pick(
            layer, layers, owned, groups, table, scalars, states, weight_tiles
        )
        weights = weights or [weight_tiles]
        incoming = lax.all_to_all(outgoing, FETCH_OVER, 0, 0, tiled=True)
        incoming = incoming.reshape(2 * rest, groups, owned + 1, 2, rows, side)
        result = multiply(layer, last, where, counts, incoming, weights, bias_terms)
        result = result.reshape((4 * rest,) + result.shape[3:])
        returned = lax.all_to_all(result, ROWS_OVER, 0, 0, tiled=True)
        state = returned.reshape((blocks,) + returned.shape[2:])
    return jnp.transpose(state, (1, 0, 2)).reshape(rows, blocks * side)


def solution(mesh):
    across, groups = mesh.shape["gx"], mesh.shape["gy"]
    split = Mesh(mesh.devices.reshape(2, 2, across // 4, groups), (HALF, PAIR, REST, GROUP))
    placed = (
        P(ROWS_OVER, GROUP),
        P(None, ROWS_OVER, GROUP),
        P(),
        P(None, GROUP, ROWS_OVER),
        P(None, GROUP, ROWS_OVER, None, None, None),
        P(None, GROUP, ROWS_OVER, None),
    )
    return jax.shard_map(
        local, mesh=split, in_specs=placed, out_specs=P(ROWS_OVER, GROUP), check_vma=False
    )
```

```python
import functools

import jax
import jax.numpy as jnp
from jax import lax
from jax.experimental import pallas as pl
from jax.experimental.pallas import tpu as pltpu
from jax.sharding import Mesh, PartitionSpec as P

HALF, PAIR, REST, GROUP = "half", "pair", "rest", "gy"
ROWS_OVER = (HALF, PAIR, REST)
FETCH_OVER = (PAIR, REST, GROUP)


def masked(alive, tile):
    return jnp.where(alive > 0, tile, jnp.zeros_like(tile))


def announce_kernel(layers, groups, counts, heavy_ref):
    lane = lax.broadcasted_iota(jnp.int32, heavy_ref.shape[1:], 1)
    found = jnp.zeros_like(lane)
    for layer in range(layers):
        found = jnp.where(lane == layer, heavy_of(counts, layer, groups), found)
    heavy_ref[...] = jnp.broadcast_to(found[None], heavy_ref.shape)


def heavy_of(counts, layer, groups):
    heavy = jnp.int32(0)
    for k in range(counts.shape[1]):
        heavy = jnp.where(counts[layer, k] > groups, k, heavy)
    return heavy


def announce(groups, devices, side, counts):
    return pl.pallas_call(
        functools.partial(announce_kernel, counts.shape[0], groups),
        out_shape=jax.ShapeDtypeStruct((devices, 1, side), jnp.int32),
        grid_spec=pltpu.PrefetchScalarGridSpec(
            num_scalar_prefetch=1,
            grid=(1,),
            in_specs=[],
            out_specs=pl.BlockSpec((devices, 1, side), lambda i, *_: (0, 0, 0)),
        ),
        compiler_params=pltpu.CompilerParams(vmem_limit_bytes=4 << 20),
        name="announce",
    )(counts)


def mask_kernel(live, rows_ref, own_ref):
    batch = 8

    def mask(b, carry):
        first = b * batch
        kept = [masked(live[first + i], rows_ref[first + i]) for i in range(batch)]
        for i in range(batch):
            own_ref[first + i] = kept[i]
        return carry

    lax.fori_loop(0, rows_ref.shape[0] // batch, mask, 0)


def mask(live, own):
    live, own = (pltpu.with_memory_space_constraint(x, pltpu.HBM) for x in (live, own))
    spec = pl.BlockSpec(own.shape, lambda i, *_: (0, 0, 0))
    return pl.pallas_call(
        mask_kernel,
        out_shape=jax.ShapeDtypeStruct(own.shape, own.dtype),
        grid_spec=pltpu.PrefetchScalarGridSpec(
            num_scalar_prefetch=1, grid=(1,), in_specs=[spec], out_specs=spec
        ),
        compiler_params=pltpu.CompilerParams(vmem_limit_bytes=4 << 20),
        name="mask",
    )(live, own)


def pick_kernel(layer, layers, owned, groups, where, table, heavy, *refs):
    half = where[0]
    batch = 8
    *live_refs, out_ref, kept_ref = refs
    blocks = kept_ref.shape[0]

    def mask(b, carry):
        first = b * batch
        kept = []
        for i in range(batch):
            spot = layer * blocks + first + i
            if layer == 0:
                live_partner, own_ref, partner_ref = live_refs
                kept.append(own_ref[first + i])
                kept.append(masked(live_partner[spot], partner_ref[first + i]))
            else:
                live_own, live_partner, state_ref = live_refs
                kept.append(masked(live_own[spot], state_ref[first + i, half]))
                kept.append(masked(live_partner[spot], state_ref[first + i, 1 - half]))
        for i in range(batch):
            kept_ref[first + i, half] = kept[2 * i]
            kept_ref[first + i, 1 - half] = kept[2 * i + 1]
        return carry

    lax.fori_loop(0, blocks // batch, mask, 0)

    across = out_ref.shape[0] // groups
    slots = table.shape[0] // (2 * layers)

    def one_owner(owner, carry):
        for g in range(groups):
            first = 2 * layer * slots + g * blocks + (half * across + owner) * owned
            spots = [table[first + k] for k in range(owned)]
            spots.append(table[first + slots + heavy[owner * groups + g, layer]])
            for k, spot in enumerate(spots):
                out_ref[owner * groups + g, k] = kept_ref[spot]
        return carry

    lax.fori_loop(0, across, one_owner, 0)


def whole(shape):
    return pl.BlockSpec(shape, lambda i, *_: (0,) * len(shape))


def pick(layer, layers, owned, groups, scalars, states, cost):
    blocks, (rows, side) = states[0].shape[0], states[0].shape[-2:]
    devices = scalars[2].shape[0]
    shape = (devices, owned + 1, 2, rows, side)
    return pl.pallas_call(
        functools.partial(pick_kernel, layer, layers, owned, groups),
        out_shape=jax.ShapeDtypeStruct(shape, states[0].dtype),
        grid_spec=pltpu.PrefetchScalarGridSpec(
            num_scalar_prefetch=len(scalars),
            grid=(1,),
            in_specs=[whole(state.shape) for state in states],
            out_specs=whole(shape),
            scratch_shapes=[pltpu.VMEM((blocks, 2, rows, side), states[0].dtype)],
        ),
        compiler_params=pltpu.CompilerParams(vmem_limit_bytes=6 << 20),
        cost_estimate=cost,
    )(*scalars, *states)


def multiply_kernel(layer, last, where, counts, x_ref, w_ref, bias_ref, out_ref, acc_ref):
    across, groups, _, _, rows, side = x_ref.shape
    owned = counts.shape[1]
    total_rows = across * 2 * rows
    half = where[0]
    heavy = heavy_of(counts, layer, groups)

    def gathered(position, first, count):
        parts = []
        for g in range(groups):
            part = x_ref[:, g, position].reshape(total_rows, side)
            parts.append(jnp.where(first + g < count, part, jnp.zeros_like(part)))
        return jnp.concatenate(parts, axis=1)

    def write(k, summed):
        value = jnp.maximum(summed, 0.0).astype(out_ref.dtype)
        value = value.reshape(2, across // 2, 2, rows, side)
        if last:
            low, high = value[:, :, 0], value[:, :, 1]
            near = jnp.where(half == 0, low, high)
            far = jnp.where(half == 0, high, low)
        else:
            near = far = value
        out_ref[half, :, :, k] = near
        out_ref[1 - half, 0, :, k] = far[1]
        out_ref[1 - half, 1, :, k] = far[0]

    def product(position, first, count, weight):
        weight = weight.reshape(groups * side, side)
        lhs = gathered(position, first, count)
        return jnp.dot(lhs, weight, preferred_element_type=jnp.float32)

    for k in range(owned):
        weight = w_ref[layer, 0, k, :groups]
        summed = product(k, 0, counts[layer, k], weight) + bias_ref[0, 0, k : k + 1, :]
        acc_ref[k] = summed
        write(k, summed)

    weight = w_ref[layer, 0, heavy, groups:]
    write(heavy, acc_ref[heavy] + product(owned, groups, counts[layer, heavy], weight))


def multiply(layer, last, where, counts, incoming, weight_tiles, bias_terms):
    across, _, width, _, rows, side = incoming.shape
    owned = width - 1
    out = (2, 2, across // 2, owned) + (() if last else (2,)) + (rows, side)
    return pl.pallas_call(
        functools.partial(multiply_kernel, layer, last),
        out_shape=jax.ShapeDtypeStruct(out, incoming.dtype),
        grid_spec=pltpu.PrefetchScalarGridSpec(
            num_scalar_prefetch=2,
            grid=(1,),
            in_specs=[
                whole(incoming.shape),
                whole(weight_tiles.shape),
                pl.BlockSpec((1, 1, owned, side), lambda i, *_: (layer, 0, 0, 0)),
            ],
            out_specs=whole(out),
            scratch_shapes=[pltpu.VMEM((owned, across * 2 * rows, side), jnp.float32)],
        ),
        compiler_params=pltpu.CompilerParams(vmem_limit_bytes=24 << 20),
    )(where, counts, incoming, weight_tiles, bias_terms)


def local(activations, live_blocks, tile_index, tile_count, weight_tiles, bias_terms):
    rest = lax.axis_size(REST)
    groups = lax.axis_size(GROUP)
    my_group = lax.axis_index(GROUP)
    my_half = lax.axis_index(HALF)
    layers = tile_index.shape[0]
    rows = activations.shape[0]
    side = weight_tiles.shape[-1]
    owned = weight_tiles.shape[2]
    blocks = activations.shape[1] // side
    devices = 2 * rest * groups
    partners = [
        ((h * 2 + p) * rest + r, ((1 - h) * 2 + 1 - p) * rest + r)
        for h in range(2)
        for p in range(2)
        for r in range(rest)
    ]

    counts = tile_count[:, 0]
    live = live_blocks[:, 0]
    own = jnp.transpose(activations.reshape(rows, blocks, side), (1, 0, 2))
    partner = lax.ppermute(own, ROWS_OVER, partners)
    counts_hbm = pltpu.with_memory_space_constraint(counts, pltpu.HBM)
    heavy = announce(groups, devices, side, counts_hbm)
    heavy = lax.all_to_all(heavy, FETCH_OVER, 0, 0, tiled=True)
    heavy = heavy[:, 0, :layers]
    live_own = live.reshape(-1)
    live_partner = lax.ppermute(live, ROWS_OVER, partners)
    live_partner = live_partner.reshape(-1)
    own = mask(live_own, own)
    where = my_half.reshape(1)

    slots = jnp.transpose(tile_index, (0, 2, 1)).reshape(layers, -1, groups, tile_index.shape[1])
    table = lax.dynamic_index_in_dim(slots, my_group, 2, keepdims=False) - my_group * blocks
    table = table.reshape(-1)

    for layer in range(layers):
        last = layer == layers - 1
        if layer == 0:
            scalars, states = (where, table, heavy, live_partner), (own, partner)
            cost = pl.CostEstimate(flops=10**11, transcendentals=0, bytes_accessed=64 << 20)
        else:
            scalars, states = (where, table, heavy, live_own, live_partner), (state,)
            cost = None
        outgoing = pick(layer, layers, owned, groups, scalars, states, cost)
        incoming = lax.all_to_all(outgoing, FETCH_OVER, 0, 0, tiled=True)
        incoming = incoming.reshape(2 * rest, groups, owned + 1, 2, rows, side)
        result = multiply(layer, last, where, counts, incoming, weight_tiles, bias_terms)
        result = result.reshape((4 * rest,) + result.shape[3:])
        returned = lax.all_to_all(result, ROWS_OVER, 0, 0, tiled=True)
        state = returned.reshape((blocks,) + returned.shape[2:])
    return jnp.transpose(state, (1, 0, 2)).reshape(rows, blocks * side)


def solution(mesh):
    across, groups = mesh.shape["gx"], mesh.shape["gy"]
    split = Mesh(mesh.devices.reshape(2, 2, across // 4, groups), (HALF, PAIR, REST, GROUP))
    placed = (
        P(ROWS_OVER, GROUP),
        P(None, ROWS_OVER, GROUP),
        P(),
        P(None, GROUP, ROWS_OVER),
        P(None, GROUP, ROWS_OVER, None, None, None),
        P(None, GROUP, ROWS_OVER, None),
    )
    return jax.shard_map(
        local, mesh=split, in_specs=placed, out_specs=P(ROWS_OVER, GROUP), check_vma=False
    )
```

```python
import functools

import jax
import jax.numpy as jnp
from jax import lax
from jax.experimental import pallas as pl
from jax.experimental.pallas import tpu as pltpu
from jax.sharding import Mesh, PartitionSpec as P

HALF, PAIR, REST, GROUP = "half", "pair", "rest", "gy"
ROWS_OVER = (HALF, PAIR, REST)
FETCH_OVER = (PAIR, REST, GROUP)


def masked(alive, tile):
    return jnp.where(alive > 0, tile, jnp.zeros_like(tile))


def announce_kernel(layers, groups, counts, heavy_ref):
    lane = lax.broadcasted_iota(jnp.int32, heavy_ref.shape[1:], 1)
    found = jnp.zeros_like(lane)
    for layer in range(layers):
        found = jnp.where(lane == layer, heavy_of(counts, layer, groups), found)
    heavy_ref[...] = jnp.broadcast_to(found[None], heavy_ref.shape)


def heavy_of(counts, layer, groups):
    heavy = jnp.int32(0)
    for k in range(counts.shape[1]):
        heavy = jnp.where(counts[layer, k] > groups, k, heavy)
    return heavy


def announce(groups, devices, side, counts):
    return pl.pallas_call(
        functools.partial(announce_kernel, counts.shape[0], groups),
        out_shape=jax.ShapeDtypeStruct((devices, 1, side), jnp.int32),
        grid_spec=pltpu.PrefetchScalarGridSpec(
            num_scalar_prefetch=1,
            grid=(1,),
            in_specs=[],
            out_specs=pl.BlockSpec((devices, 1, side), lambda i, *_: (0, 0, 0)),
        ),
        compiler_params=pltpu.CompilerParams(vmem_limit_bytes=4 << 20),
        name="announce",
    )(counts)


def mask_kernel(live, rows_ref, own_ref):
    batch = 8

    def mask(b, carry):
        first = b * batch
        kept = [masked(live[first + i], rows_ref[first + i]) for i in range(batch)]
        for i in range(batch):
            own_ref[first + i] = kept[i]
        return carry

    lax.fori_loop(0, rows_ref.shape[0] // batch, mask, 0)


def mask(live, own):
    live, own = (pltpu.with_memory_space_constraint(x, pltpu.HBM) for x in (live, own))
    spec = pl.BlockSpec(own.shape, lambda i, *_: (0, 0, 0))
    return pl.pallas_call(
        mask_kernel,
        out_shape=jax.ShapeDtypeStruct(own.shape, own.dtype),
        grid_spec=pltpu.PrefetchScalarGridSpec(
            num_scalar_prefetch=1, grid=(1,), in_specs=[spec], out_specs=spec
        ),
        compiler_params=pltpu.CompilerParams(vmem_limit_bytes=4 << 20),
        name="mask",
    )(live, own)


def pick_kernel(layer, owned, groups, where, heavy, *refs):
    half = where[0]
    batch = 8
    *live_refs, table_any, out_ref, kept_ref, table, sem = refs
    slots = table.shape[0] // 2
    fetch = pltpu.make_async_copy(
        table_any.at[pl.ds(2 * layer * slots, 2 * slots)], table, sem
    )
    fetch.start()
    blocks = kept_ref.shape[0]

    def mask(b, carry):
        first = b * batch
        kept = []
        for i in range(batch):
            spot = layer * blocks + first + i
            if layer == 0:
                live_partner, own_ref, partner_ref = live_refs
                kept.append(own_ref[first + i])
                kept.append(masked(live_partner[spot], partner_ref[first + i]))
            else:
                live_own, live_partner, state_ref = live_refs
                kept.append(masked(live_own[spot], state_ref[first + i, half]))
                kept.append(masked(live_partner[spot], state_ref[first + i, 1 - half]))
        for i in range(batch):
            kept_ref[first + i, half] = kept[2 * i]
            kept_ref[first + i, 1 - half] = kept[2 * i + 1]
        return carry

    lax.fori_loop(0, blocks // batch, mask, 0)

    across = out_ref.shape[0] // groups
    fetch.wait()

    def one_owner(owner, carry):
        for g in range(groups):
            first = g * blocks + (half * across + owner) * owned
            spots = [table[first + k] for k in range(owned)]
            spots.append(table[first + slots + heavy[owner * groups + g, layer]])
            for k, spot in enumerate(spots):
                out_ref[owner * groups + g, k] = kept_ref[spot]
        return carry

    lax.fori_loop(0, across, one_owner, 0)


def whole(shape):
    return pl.BlockSpec(shape, lambda i, *_: (0,) * len(shape))


def pick(layer, layers, owned, groups, scalars, states, table, cost):
    blocks, (rows, side) = states[0].shape[0], states[0].shape[-2:]
    devices = scalars[1].shape[0]
    shape = (devices, owned + 1, 2, rows, side)
    return pl.pallas_call(
        functools.partial(pick_kernel, layer, owned, groups),
        out_shape=jax.ShapeDtypeStruct(shape, states[0].dtype),
        grid_spec=pltpu.PrefetchScalarGridSpec(
            num_scalar_prefetch=len(scalars),
            grid=(1,),
            in_specs=[whole(state.shape) for state in states] + [pl.BlockSpec(memory_space=pl.ANY)],
            out_specs=whole(shape),
            scratch_shapes=[
                pltpu.VMEM((blocks, 2, rows, side), states[0].dtype),
                pltpu.SMEM((table.shape[0] // layers,), jnp.int32),
                pltpu.SemaphoreType.DMA,
            ],
        ),
        compiler_params=pltpu.CompilerParams(vmem_limit_bytes=6 << 20),
        cost_estimate=cost,
    )(*scalars, *states, table)


def multiply_kernel(layer, last, where, counts, x_ref, w_ref, bias_ref, out_ref, acc_ref):
    across, groups, _, _, rows, side = x_ref.shape
    owned = counts.shape[1]
    total_rows = across * 2 * rows
    half = where[0]
    heavy = heavy_of(counts, layer, groups)

    def gathered(position, first, count):
        parts = []
        for g in range(groups):
            part = x_ref[:, g, position].reshape(total_rows, side)
            parts.append(jnp.where(first + g < count, part, jnp.zeros_like(part)))
        return jnp.concatenate(parts, axis=1)

    def write(k, summed):
        value = jnp.maximum(summed, 0.0).astype(out_ref.dtype)
        value = value.reshape(2, across // 2, 2, rows, side)
        if last:
            low, high = value[:, :, 0], value[:, :, 1]
            near = jnp.where(half == 0, low, high)
            far = jnp.where(half == 0, high, low)
        else:
            near = far = value
        out_ref[half, :, :, k] = near
        out_ref[1 - half, 0, :, k] = far[1]
        out_ref[1 - half, 1, :, k] = far[0]

    def product(position, first, count, weight):
        weight = weight.reshape(groups * side, side)
        lhs = gathered(position, first, count)
        return jnp.dot(lhs, weight, preferred_element_type=jnp.float32)

    for k in range(owned):
        weight = w_ref[layer, 0, k, :groups]
        summed = product(k, 0, counts[layer, k], weight) + bias_ref[0, 0, k : k + 1, :]
        acc_ref[k] = summed
        write(k, summed)

    weight = w_ref[layer, 0, heavy, groups:]
    write(heavy, acc_ref[heavy] + product(owned, groups, counts[layer, heavy], weight))


def multiply(layer, last, where, counts, incoming, weight_tiles, bias_terms):
    across, _, width, _, rows, side = incoming.shape
    owned = width - 1
    out = (2, 2, across // 2, owned) + (() if last else (2,)) + (rows, side)
    return pl.pallas_call(
        functools.partial(multiply_kernel, layer, last),
        out_shape=jax.ShapeDtypeStruct(out, incoming.dtype),
        grid_spec=pltpu.PrefetchScalarGridSpec(
            num_scalar_prefetch=2,
            grid=(1,),
            in_specs=[
                whole(incoming.shape),
                whole(weight_tiles.shape),
                pl.BlockSpec((1, 1, owned, side), lambda i, *_: (layer, 0, 0, 0)),
            ],
            out_specs=whole(out),
            scratch_shapes=[pltpu.VMEM((owned, across * 2 * rows, side), jnp.float32)],
        ),
        compiler_params=pltpu.CompilerParams(vmem_limit_bytes=24 << 20),
    )(where, counts, incoming, weight_tiles, bias_terms)


def local(activations, live_blocks, tile_index, tile_count, weight_tiles, bias_terms):
    rest = lax.axis_size(REST)
    groups = lax.axis_size(GROUP)
    my_group = lax.axis_index(GROUP)
    my_half = lax.axis_index(HALF)
    layers = tile_index.shape[0]
    rows = activations.shape[0]
    side = weight_tiles.shape[-1]
    owned = weight_tiles.shape[2]
    blocks = activations.shape[1] // side
    devices = 2 * rest * groups
    partners = [
        ((h * 2 + p) * rest + r, ((1 - h) * 2 + 1 - p) * rest + r)
        for h in range(2)
        for p in range(2)
        for r in range(rest)
    ]

    counts = tile_count[:, 0]
    live = live_blocks[:, 0]
    own = jnp.transpose(activations.reshape(rows, blocks, side), (1, 0, 2))
    partner = lax.ppermute(own, ROWS_OVER, partners)
    counts_hbm = pltpu.with_memory_space_constraint(counts, pltpu.HBM)
    heavy = announce(groups, devices, side, counts_hbm)
    heavy = lax.all_to_all(heavy, FETCH_OVER, 0, 0, tiled=True)
    heavy = heavy[:, 0, :layers]
    live_own = live.reshape(-1)
    live_partner = lax.ppermute(live, ROWS_OVER, partners)
    live_partner = live_partner.reshape(-1)
    own = mask(live_own, own)
    where = my_half.reshape(1)

    slots = jnp.transpose(tile_index, (0, 2, 1)).reshape(layers, -1, groups, tile_index.shape[1])
    table = lax.dynamic_index_in_dim(slots, my_group, 2, keepdims=False) - my_group * blocks
    table = table.reshape(-1)

    for layer in range(layers):
        last = layer == layers - 1
        if layer == 0:
            scalars, states = (where, heavy, live_partner), (own, partner)
            cost = pl.CostEstimate(flops=10**11, transcendentals=0, bytes_accessed=64 << 20)
        else:
            scalars, states = (where, heavy, live_own, live_partner), (state,)
            cost = None
        outgoing = pick(layer, layers, owned, groups, scalars, states, table, cost)
        incoming = lax.all_to_all(outgoing, FETCH_OVER, 0, 0, tiled=True)
        incoming = incoming.reshape(2 * rest, groups, owned + 1, 2, rows, side)
        result = multiply(layer, last, where, counts, incoming, weight_tiles, bias_terms)
        result = result.reshape((4 * rest,) + result.shape[3:])
        returned = lax.all_to_all(result, ROWS_OVER, 0, 0, tiled=True)
        state = returned.reshape((blocks,) + returned.shape[2:])
    return jnp.transpose(state, (1, 0, 2)).reshape(rows, blocks * side)


def solution(mesh):
    across, groups = mesh.shape["gx"], mesh.shape["gy"]
    split = Mesh(mesh.devices.reshape(2, 2, across // 4, groups), (HALF, PAIR, REST, GROUP))
    placed = (
        P(ROWS_OVER, GROUP),
        P(None, ROWS_OVER, GROUP),
        P(),
        P(None, GROUP, ROWS_OVER),
        P(None, GROUP, ROWS_OVER, None, None, None),
        P(None, GROUP, ROWS_OVER, None),
    )
    return jax.shard_map(
        local, mesh=split, in_specs=placed, out_specs=P(ROWS_OVER, GROUP), check_vma=False
    )
```

```python
import functools

import jax
import jax.numpy as jnp
from jax import lax
from jax.experimental import pallas as pl
from jax.experimental.pallas import tpu as pltpu
from jax.sharding import Mesh, PartitionSpec as P

HALF, PAIR, REST, GROUP = "half", "pair", "rest", "gy"
ROWS_OVER = (HALF, PAIR, REST)
FETCH_OVER = (PAIR, REST, GROUP)


def masked(alive, tile):
    return tile * jnp.full(tile.shape, alive.astype(jnp.float32)).astype(tile.dtype)


def announce_kernel(layers, groups, counts, heavy_ref):
    lane = lax.broadcasted_iota(jnp.int32, heavy_ref.shape[1:], 1)
    found = jnp.zeros_like(lane)
    for layer in range(layers):
        found = jnp.where(lane == layer, heavy_of(counts, layer, groups), found)
    heavy_ref[...] = jnp.broadcast_to(found[None], heavy_ref.shape)


def heavy_of(counts, layer, groups):
    heavy = jnp.int32(0)
    for k in range(counts.shape[1]):
        heavy = jnp.where(counts[layer, k] > groups, k, heavy)
    return heavy


def announce(groups, devices, side, counts):
    return pl.pallas_call(
        functools.partial(announce_kernel, counts.shape[0], groups),
        out_shape=jax.ShapeDtypeStruct((devices, 1, side), jnp.int32),
        grid_spec=pltpu.PrefetchScalarGridSpec(
            num_scalar_prefetch=1,
            grid=(1,),
            in_specs=[],
            out_specs=pl.BlockSpec((devices, 1, side), lambda i, *_: (0, 0, 0)),
        ),
        compiler_params=pltpu.CompilerParams(vmem_limit_bytes=4 << 20),
        name="announce",
    )(counts)


def mask_kernel(live, rows_ref, own_ref):
    batch = 32

    def mask(b, carry):
        first = b * batch
        kept = [masked(live[first + i], rows_ref[first + i]) for i in range(batch)]
        for i in range(batch):
            own_ref[first + i] = kept[i]
        return carry

    lax.fori_loop(0, rows_ref.shape[0] // batch, mask, 0)


def mask(live, own):
    live, own = (pltpu.with_memory_space_constraint(x, pltpu.HBM) for x in (live, own))
    spec = pl.BlockSpec(own.shape, lambda i, *_: (0, 0, 0))
    return pl.pallas_call(
        mask_kernel,
        out_shape=jax.ShapeDtypeStruct(own.shape, own.dtype),
        grid_spec=pltpu.PrefetchScalarGridSpec(
            num_scalar_prefetch=1, grid=(1,), in_specs=[spec], out_specs=spec
        ),
        compiler_params=pltpu.CompilerParams(vmem_limit_bytes=4 << 20),
        name="mask",
    )(live, own)


def pick_kernel(layer, owned, groups, where, heavy, *refs):
    half = where[0]
    batch = 32
    *live_refs, table_any, out_ref, kept_ref, table, sem = refs
    slots = table.shape[0] // 2
    fetch = pltpu.make_async_copy(
        table_any.at[pl.ds(2 * layer * slots, 2 * slots)], table, sem
    )
    fetch.start()
    blocks = kept_ref.shape[0]

    def mask(b, carry):
        first = b * batch
        kept = []
        for i in range(batch):
            spot = layer * blocks + first + i
            if layer == 0:
                live_partner, own_ref, partner_ref = live_refs
                kept.append(own_ref[first + i])
                kept.append(masked(live_partner[spot], partner_ref[first + i]))
            else:
                live_own, live_partner, state_ref = live_refs
                kept.append(masked(live_own[spot], state_ref[first + i, half]))
                kept.append(masked(live_partner[spot], state_ref[first + i, 1 - half]))
        for i in range(batch):
            kept_ref[first + i, half] = kept[2 * i]
            kept_ref[first + i, 1 - half] = kept[2 * i + 1]
        return carry

    lax.fori_loop(0, blocks // batch, mask, 0)

    across = out_ref.shape[0] // groups
    fetch.wait()

    def one_owner(owner, carry):
        for g in range(groups):
            first = g * blocks + (half * across + owner) * owned
            spots = [table[first + k] for k in range(owned)]
            spots.append(table[first + slots + heavy[owner * groups + g, layer]])
            for k, spot in enumerate(spots):
                out_ref[owner * groups + g, k] = kept_ref[spot]
        return carry

    lax.fori_loop(0, across, one_owner, 0)


def whole(shape):
    return pl.BlockSpec(shape, lambda i, *_: (0,) * len(shape))


def pick(layer, layers, owned, groups, scalars, states, table, cost):
    blocks, (rows, side) = states[0].shape[0], states[0].shape[-2:]
    devices = scalars[1].shape[0]
    shape = (devices, owned + 1, 2, rows, side)
    return pl.pallas_call(
        functools.partial(pick_kernel, layer, owned, groups),
        out_shape=jax.ShapeDtypeStruct(shape, states[0].dtype),
        grid_spec=pltpu.PrefetchScalarGridSpec(
            num_scalar_prefetch=len(scalars),
            grid=(1,),
            in_specs=[whole(state.shape) for state in states] + [pl.BlockSpec(memory_space=pl.ANY)],
            out_specs=whole(shape),
            scratch_shapes=[
                pltpu.VMEM((blocks, 2, rows, side), states[0].dtype),
                pltpu.SMEM((table.shape[0] // layers,), jnp.int32),
                pltpu.SemaphoreType.DMA,
            ],
        ),
        compiler_params=pltpu.CompilerParams(vmem_limit_bytes=6 << 20),
        cost_estimate=cost,
    )(*scalars, *states, table)


def multiply_kernel(layer, last, where, counts, x_ref, w_ref, bias_ref, out_ref, acc_ref):
    across, groups, _, _, rows, side = x_ref.shape
    owned = counts.shape[1]
    total_rows = across * 2 * rows
    half = where[0]
    heavy = heavy_of(counts, layer, groups)

    def gathered(position, first, count):
        parts = []
        for g in range(groups):
            part = x_ref[:, g, position].reshape(total_rows, side)
            parts.append(jnp.where(first + g < count, part, jnp.zeros_like(part)))
        return jnp.concatenate(parts, axis=1)

    def write(k, summed):
        value = jnp.maximum(summed, 0.0).astype(out_ref.dtype)
        value = value.reshape(2, across // 2, 2, rows, side)
        if last:
            low, high = value[:, :, 0], value[:, :, 1]
            near = jnp.where(half == 0, low, high)
            far = jnp.where(half == 0, high, low)
        else:
            near = far = value
        out_ref[half, :, :, k] = near
        out_ref[1 - half, 0, :, k] = far[1]
        out_ref[1 - half, 1, :, k] = far[0]

    def product(position, first, count, weight):
        weight = weight.reshape(groups * side, side)
        lhs = gathered(position, first, count)
        return jnp.dot(lhs, weight, preferred_element_type=jnp.float32)

    for k in range(owned):
        weight = w_ref[layer, 0, k, :groups]
        summed = product(k, 0, counts[layer, k], weight) + bias_ref[0, 0, k : k + 1, :]
        acc_ref[k] = summed
        write(k, summed)

    weight = w_ref[layer, 0, heavy, groups:]
    write(heavy, acc_ref[heavy] + product(owned, groups, counts[layer, heavy], weight))


def multiply(layer, last, where, counts, incoming, weight_tiles, bias_terms):
    across, _, width, _, rows, side = incoming.shape
    owned = width - 1
    out = (2, 2, across // 2, owned) + (() if last else (2,)) + (rows, side)
    return pl.pallas_call(
        functools.partial(multiply_kernel, layer, last),
        out_shape=jax.ShapeDtypeStruct(out, incoming.dtype),
        grid_spec=pltpu.PrefetchScalarGridSpec(
            num_scalar_prefetch=2,
            grid=(1,),
            in_specs=[
                whole(incoming.shape),
                whole(weight_tiles.shape),
                pl.BlockSpec((1, 1, owned, side), lambda i, *_: (layer, 0, 0, 0)),
            ],
            out_specs=whole(out),
            scratch_shapes=[pltpu.VMEM((owned, across * 2 * rows, side), jnp.float32)],
        ),
        compiler_params=pltpu.CompilerParams(vmem_limit_bytes=24 << 20),
    )(where, counts, incoming, weight_tiles, bias_terms)


def local(activations, live_blocks, tile_index, tile_count, weight_tiles, bias_terms):
    rest = lax.axis_size(REST)
    groups = lax.axis_size(GROUP)
    my_group = lax.axis_index(GROUP)
    my_half = lax.axis_index(HALF)
    layers = tile_index.shape[0]
    rows = activations.shape[0]
    side = weight_tiles.shape[-1]
    owned = weight_tiles.shape[2]
    blocks = activations.shape[1] // side
    devices = 2 * rest * groups
    partners = [
        ((h * 2 + p) * rest + r, ((1 - h) * 2 + 1 - p) * rest + r)
        for h in range(2)
        for p in range(2)
        for r in range(rest)
    ]

    counts = tile_count[:, 0]
    live = live_blocks[:, 0]
    own = jnp.transpose(activations.reshape(rows, blocks, side), (1, 0, 2))
    partner = lax.ppermute(own, ROWS_OVER, partners)
    counts_hbm = pltpu.with_memory_space_constraint(counts, pltpu.HBM)
    heavy = announce(groups, devices, side, counts_hbm)
    heavy = lax.all_to_all(heavy, FETCH_OVER, 0, 0, tiled=True)
    heavy = heavy[:, 0, :layers]
    live_own = live.reshape(-1)
    live_partner = lax.ppermute(live, ROWS_OVER, partners)
    live_partner = live_partner.reshape(-1)
    own = mask(live_own, own)
    where = my_half.reshape(1)

    slots = jnp.transpose(tile_index, (0, 2, 1)).reshape(layers, -1, groups, tile_index.shape[1])
    table = lax.dynamic_index_in_dim(slots, my_group, 2, keepdims=False) - my_group * blocks
    table = table.reshape(-1)

    for layer in range(layers):
        last = layer == layers - 1
        if layer == 0:
            scalars, states = (where, heavy, live_partner), (own, partner)
            cost = pl.CostEstimate(flops=10**11, transcendentals=0, bytes_accessed=64 << 20)
        else:
            scalars, states = (where, heavy, live_own, live_partner), (state,)
            cost = None
        outgoing = pick(layer, layers, owned, groups, scalars, states, table, cost)
        incoming = lax.all_to_all(outgoing, FETCH_OVER, 0, 0, tiled=True)
        incoming = incoming.reshape(2 * rest, groups, owned + 1, 2, rows, side)
        result = multiply(layer, last, where, counts, incoming, weight_tiles, bias_terms)
        result = result.reshape((4 * rest,) + result.shape[3:])
        returned = lax.all_to_all(result, ROWS_OVER, 0, 0, tiled=True)
        state = returned.reshape((blocks,) + returned.shape[2:])
    return jnp.transpose(state, (1, 0, 2)).reshape(rows, blocks * side)


def solution(mesh):
    across, groups = mesh.shape["gx"], mesh.shape["gy"]
    split = Mesh(mesh.devices.reshape(2, 2, across // 4, groups), (HALF, PAIR, REST, GROUP))
    placed = (
        P(ROWS_OVER, GROUP),
        P(None, ROWS_OVER, GROUP),
        P(),
        P(None, GROUP, ROWS_OVER),
        P(None, GROUP, ROWS_OVER, None, None, None),
        P(None, GROUP, ROWS_OVER, None),
    )
    return jax.shard_map(
        local, mesh=split, in_specs=placed, out_specs=P(ROWS_OVER, GROUP), check_vma=False
    )
```
